256 devices in a mesh: expert: 64 (over y, z, core), tensor: 4 (over x).
Axes of the slice: x: 4, y: 4, z: 8, core: 2. Of those that a mesh axis runs over, the one named last changes fastest.
Arguments:
- tokens: bfloat16 [8192, 2048], P('expert', 'tensor'), may hold values from -6 to 6
- grad_out: bfloat16 [8192, 2048], P('expert', 'tensor'), may hold values from -6 to 6
- gates: float32 [8192, 6], P('expert'), may hold values from 0.1 to 1
- expert_ids: int32 [8192, 6], P('expert'), may hold values from 0 to 63, all different within a row; in each aligned block of 128 rows (0 to 127, 128 to 255, ...) at most 16 rows name the same one
- w_gate: bfloat16 [64, 2048, 1408], P('expert', None, 'tensor'), may hold values from -0.125 to 0.125
- w_up: bfloat16 [64, 2048, 1408], P('expert', None, 'tensor'), may hold values from -0.125 to 0.125
- w_down: bfloat16 [64, 1408, 2048], P('expert', 'tensor'), may hold values from -0.15625 to 0.15625
Outputs:
- mixed: bfloat16 [8192, 2048], P('expert', 'tensor')
- grad_tokens: bfloat16 [8192, 2048], P('expert', 'tensor')
- grad_gates: float32 [8192, 6], P('expert')
- grad_w_gate: bfloat16 [64, 2048, 1408], P('expert', None, 'tensor')
- grad_w_up: bfloat16 [64, 2048, 1408], P('expert', None, 'tensor')
- grad_w_down: bfloat16 [64, 1408, 2048], P('expert', 'tensor')
The draws below stay inside these ranges and needn't reach their ends.
Inputs may be any that keep to these rules, and one draw needn't show every extreme that they name: `expert_ids`: each row names 6 different experts. In each aligned block of 128 rows (the tokens of one index of expert) no expert is named by more than 16 rows, and some block names some expert exactly 16 times.
All inputs are finite; a program needn't handle non-finite values.
Results may differ from the reference program's by a relative error of at most 0.0064.
Values may be sent and summed in bfloat16 or wider, within the bound.
A program may use at most 128 MiB of HBM per device.

```python
import math
import jax
import jax.numpy as jnp
import numpy as np
from jax import lax

D = 2048
FF = 1408
TOP = 6
TOK_DEV = 128
EXPERTS = 64
TOKENS = 8192
CAP = 16
EXPERT_ROWS = 1024


def block_scale(stream_key, extent, cuts, smallest, high):
    level, own = 1.0, jax.random.fold_in(stream_key, 6)
    for dim, shards_of in cuts:
        heights = jnp.exp(jax.random.uniform(jax.random.fold_in(own, dim), (shards_of,), jnp.float32, smallest / len(cuts), high / len(cuts)))
        level = level * jnp.repeat(heights, extent[dim] // shards_of).reshape([-1 if axis == dim else 1 for axis in range(len(extent))])
    return level


def deal_out(rng, own, number, rows, count, top, reach, slope):
    ranking = jax.random.permutation(rng, count)
    packed, usual = shares(count, rows * top, reach, slope, True), shares(count, rows * top, reach, slope, False)
    places = jnp.arange(count)

    def named(sizes, offset_by):
        used = int((sizes > 0).sum())
        fixed = max(1, used // 4)
        moved = fixed + (places - fixed + offset_by * (used - fixed)) % max(1, count - fixed)
        return jnp.zeros((count,), jnp.int32).at[ranking[jnp.where(places < fixed, places, moved)]].set(jnp.asarray(sizes, jnp.int32))

    sizes = jnp.where(number % 4 == 0, named(packed, number // 4), named(usual, number - number // 4 - 1))
    mixed = jax.random.permutation(jax.random.fold_in(own, 3), count)
    giver, sink = mixed[0:count // 2 * 2:2], mixed[1:count // 2 * 2:2]
    room = jnp.minimum(sizes[giver] - 1, reach - sizes[sink]) // 2
    room = jnp.where((giver == ranking[0]) | (sink == ranking[0]) | (sizes[sink] == 0), 0, jnp.maximum(room, 0))
    moved = jax.random.randint(jax.random.fold_in(own, 4), (count // 2,), 0, 1 << 20) % (room + 1)
    sizes = sizes.at[giver].add(-moved).at[sink].add(moved)
    items = jnp.searchsorted(jnp.cumsum(sizes), jnp.arange(rows * top), side="right").astype(jnp.int32)
    table = items.reshape(top, rows).T
    table = table[jax.random.permutation(jax.random.fold_in(own, 1), rows)]
    offset_by = jax.random.randint(jax.random.fold_in(own, 2), (rows, 1), 0, top)
    return jnp.take_along_axis(table, (jnp.arange(top)[None, :] + offset_by) % top, axis=1)


def shares(amount, total, limit, skew, full):
    loads = [(1 << 20) // math.isqrt(rank ** skew) + 1 for rank in range(1, amount + 1)]
    largest = limit if full else min(limit, max(-(-total // amount), total * loads[0] // sum(loads)))
    least = 1 if total - largest >= amount - 1 else 0
    holding, spare = [largest] + [least] * (amount - 1), total - largest - least * (amount - 1)
    while spare > 0:
        free = [i for i in range(1, amount) if holding[i] < largest] or [i for i in range(1, amount) if holding[i] < limit]
        mass, left = sum([loads[i] for i in free]), spare
        for i in free:
            more = min(limit - holding[i], max(1, left * loads[i] // mass), spare)
            holding[i] = holding[i] + more
            spare = spare - more
    return np.array(holding)


def bell_draw(rng, dims, deviation, bound, shards=(), kind=jnp.bfloat16):
    result = jax.random.normal(rng, dims, jnp.float32) * deviation
    if len(shards) > 0:
        result = block_scale(rng, dims, shards, -0.22, 0.18) * result
    return jnp.clip(result, min=-bound, max=bound).astype(kind)


def setup_inputs(seed: int = 0) -> dict:
    seeds = jax.random.split(jax.random.key(seed), 8)
    tokens = bell_draw(seeds[0], (TOKENS, D), 1.0, 6.0, ((0, 64), (1, 4)))
    grad_out = bell_draw(seeds[1], (TOKENS, D), 1.0, 6.0, ((0, 64), (1, 4)))
    gates = jnp.clip(jnp.exp(math.log(1.0) - 2.3025851 * jax.random.uniform(seeds[2], (TOKENS, TOP), jnp.float32) ** block_scale(seeds[2], (TOKENS, TOP), ((0, 64),), -0.2, 0.2)), 0.1, 1.0)
    expert_ids_keys = jax.random.split(jax.random.fold_in(seeds[3], 1), TOKENS // TOK_DEV)
    expert_ids_turns = jax.random.permutation(jax.random.fold_in(seeds[3], 3), TOKENS // TOK_DEV)
    expert_ids = jax.vmap(lambda own, number: deal_out(jax.random.fold_in(seeds[3], 2), own, number, TOK_DEV, EXPERTS, TOP, CAP, 1))(expert_ids_keys, expert_ids_turns).reshape((TOKENS, TOP))
    w_gate = bell_draw(seeds[4], (EXPERTS, D, FF), D ** -0.5, 0.125, ((0, 64), (2, 4)))
    w_up = bell_draw(seeds[5], (EXPERTS, D, FF), D ** -0.5, 0.125, ((0, 64), (2, 4)))
    w_down = bell_draw(seeds[6], (EXPERTS, FF, D), FF ** -0.5, 0.15625, ((0, 64), (1, 4)))
    return dict(tokens=tokens, grad_out=grad_out, gates=gates, expert_ids=expert_ids, w_gate=w_gate, w_up=w_up, w_down=w_down)


def expert_pass(rows, grad_rows, weight_gate, weight_up, weight_down):
    gate_pre = jnp.dot(rows, weight_gate, preferred_element_type=jnp.float32)
    up_pre = jnp.dot(rows, weight_up, preferred_element_type=jnp.float32)
    sig = jax.nn.sigmoid(gate_pre)
    act = (gate_pre * sig * up_pre).astype(jnp.bfloat16)
    expert_out = jnp.dot(act, weight_down, preferred_element_type=jnp.float32).astype(jnp.bfloat16)
    grad_act = jnp.dot(grad_rows, weight_down.T, preferred_element_type=jnp.float32)
    grad_gate_pre = (grad_act * up_pre * sig * (1.0 + gate_pre * (1.0 - sig))).astype(jnp.bfloat16)
    grad_up_pre = (grad_act * gate_pre * sig).astype(jnp.bfloat16)
    grad_down = jnp.dot(act.T, grad_rows, preferred_element_type=jnp.float32).astype(jnp.bfloat16)
    grad_gate = jnp.dot(rows.T, grad_gate_pre, preferred_element_type=jnp.float32).astype(jnp.bfloat16)
    grad_up = jnp.dot(rows.T, grad_up_pre, preferred_element_type=jnp.float32).astype(jnp.bfloat16)
    grad_x = (jnp.dot(grad_gate_pre, weight_gate.T, preferred_element_type=jnp.float32)
              + jnp.dot(grad_up_pre, weight_up.T, preferred_element_type=jnp.float32)).astype(jnp.bfloat16)
    return expert_out, grad_x, grad_gate, grad_up, grad_down


def reference(tokens, grad_out, gates, expert_ids, w_gate, w_up, w_down):
    pair_total = TOKENS * TOP
    flat_ids = expert_ids.reshape(-1)
    pair_token = (jnp.arange(pair_total, dtype=jnp.int32) // TOP).astype(jnp.int32)
    scaled = (gates.reshape(-1)[:, None] * grad_out[pair_token].astype(jnp.float32)).astype(grad_out.dtype)
    tokens_pad = jnp.concatenate([tokens, jnp.zeros((1, D), tokens.dtype)], axis=0)
    scaled_pad = jnp.concatenate([scaled, jnp.zeros((1, D), scaled.dtype)], axis=0)

    def one_expert(operands):
        expert_index, weight_gate, weight_up, weight_down = operands
        chosen = jnp.nonzero(flat_ids == expert_index, size=EXPERT_ROWS, fill_value=pair_total)[0].astype(jnp.int32)
        rows = tokens_pad[(chosen // TOP).astype(jnp.int32)]
        grad_rows = scaled_pad[chosen]
        results = expert_pass(rows, grad_rows, weight_gate, weight_up, weight_down)
        return results + (chosen,)

    expert_out, grad_x, grad_gate, grad_up, grad_down, chosen = lax.map(
        one_expert, (jnp.arange(EXPERTS, dtype=jnp.int32), w_gate, w_up, w_down))
    chosen = chosen.reshape(-1)
    out_pairs = jnp.zeros((pair_total + 1, D), expert_out.dtype).at[chosen].set(expert_out.reshape(-1, D))[:pair_total]
    dx_pairs = jnp.zeros((pair_total + 1, D), grad_x.dtype).at[chosen].set(grad_x.reshape(-1, D))[:pair_total]
    out_pairs = out_pairs.reshape(TOKENS, TOP, D).astype(jnp.float32)
    dx_pairs = dx_pairs.reshape(TOKENS, TOP, D).astype(jnp.float32)
    mixed = jnp.sum(gates[:, :, None] * out_pairs, axis=1).astype(tokens.dtype)
    grad_gates = jnp.sum(grad_out.astype(jnp.float32)[:, None, :] * out_pairs, axis=2)
    grad_tokens = jnp.sum(dx_pairs, axis=1).astype(tokens.dtype)
    return (mixed, grad_tokens, grad_gates, grad_gate, grad_up, grad_down)
```

```python
import functools

import jax
import jax.numpy as jnp
from jax import lax
from jax.experimental import pallas as pl
from jax.experimental.pallas import tpu as pltpu
from jax.sharding import PartitionSpec as P

F32 = jnp.float32
BF16 = jnp.bfloat16
CHUNKS = 4
AHEAD = 3
NT = (((1,), (1,)), ((), ()))
TN = (((0,), (0,)), ((), ()))


def moe_kernel(E, T, C, NC, GL, s_ref, wg_hbm, wu_hbm, wd_hbm, xg_out, act, ggp, gup, q_out, vr_out,
               xg, part, gate_s, up_s, wg, wu, wd, half_l, half_r, blk_l, blk_r, fin, vp, vx, vs,
               w_sem, out_sem, ds_sem, dr_sem, xs_sem, xr_sem, fs_sem, fr_sem, hs_sem, hr_sem,
               bs_sem, br_sem, qs_sem, qr_sem, vxs_sem, vxr_sem, vs_sem, vr_sem):
    OPC = E // NC
    CR = OPC * C
    HR = CR // 2
    W = s_ref.shape[2]
    OG = GL // C
    NG = CR // GL
    U = 2 * NC
    me = lax.axis_index("expert")
    x = lax.axis_index("tensor")
    right = lax.rem(x + 1, T)
    left = lax.rem(x + T - 1, T)
    opp = lax.rem(x + 2, T)
    xcols = pl.ds(pl.multiple_of(x * W, W), W)
    lcols = pl.ds(pl.multiple_of(left * W, W), W)
    rcols = pl.ds(pl.multiple_of(right * W, W), W)

    barrier = pltpu.get_barrier_semaphore()

    def greet(r, carry):
        pl.semaphore_signal(barrier, inc=1, device_id=(lax.rem(me + r, E), x), device_id_type=pl.DeviceIdType.MESH)
        return carry

    lax.fori_loop(1, E, greet, 0)
    for d in range(1, T):
        pl.semaphore_signal(barrier, inc=1, device_id=(me, lax.rem(x + d, T)), device_id_type=pl.DeviceIdType.MESH)
    loads = [pltpu.make_async_copy(a, b, w_sem.at[i]) for i, (a, b) in enumerate(((wg_hbm, wg), (wu_hbm, wu), (wd_hbm, wd)))]
    for load in loads:
        load.start()
    pl.semaphore_wait(barrier, E - 1 + T - 1)

    def remote(src, dst, send, recv, dev):
        return pltpu.make_async_remote_copy(src_ref=src, dst_ref=dst, send_sem=send, recv_sem=recv,
                                            device_id=dev, device_id_type=pl.DeviceIdType.MESH)

    def settle(ref, sem):
        pltpu.make_async_copy(ref, ref, sem).wait()

    def rows_of(c):
        return pl.ds(pl.multiple_of(c * CR, CR), CR)

    def first_half(c):
        return pl.ds(pl.multiple_of(c * CR, HR), HR)

    def last_half(c):
        return pl.ds(pl.multiple_of(c * CR + HR, HR), HR)

    def block(r):
        return pl.ds(pl.multiple_of(r * C, C), C)

    def dispatch(u):
        a, c = u // NC, lax.rem(u, NC)

        def one(k, carry):
            r = c * OPC + k
            to = lax.rem(me + r, E)

            @pl.when(r > 0)
            def _():
                remote(s_ref.at[a, block(to)], xg.at[a, block(r), xcols], ds_sem.at[a], dr_sem.at[u], (to, x)).start()

            @pl.when(r == 0)
            def _():
                pltpu.make_async_copy(s_ref.at[a, block(me)], xg.at[a, block(0), xcols], dr_sem.at[u]).start()

            return carry

        lax.fori_loop(0, OPC, one, 0)

    def spread(u):
        a, c = u // NC, lax.rem(u, NC)
        mine = xg.at[a, rows_of(c), xcols]
        settle(mine, dr_sem.at[u])
        remote(mine, mine, xs_sem.at[0, u], xr_sem.at[0, u], (me, right)).start()
        remote(mine, mine, xs_sem.at[1, u], xr_sem.at[1, u], (me, left)).start()

    def forward(u):
        a, c = u // NC, lax.rem(u, NC)
        settle(xg.at[a, rows_of(c), lcols], xr_sem.at[0, u])
        part_l = xg.at[a, first_half(c), lcols]
        remote(part_l, part_l, fs_sem.at[0, u], fr_sem.at[0, u], (me, right)).start()
        settle(xg.at[a, rows_of(c), rcols], xr_sem.at[1, u])
        part_r = xg.at[a, last_half(c), rcols]
        remote(part_r, part_r, fs_sem.at[1, u], fr_sem.at[1, u], (me, left)).start()

    def complete(u):
        a, c = u // NC, lax.rem(u, NC)
        ocols = pl.ds(pl.multiple_of(opp * W, W), W)
        settle(xg.at[a, first_half(c), ocols], fr_sem.at[0, u])
        settle(xg.at[a, last_half(c), ocols], fr_sem.at[1, u])
        pltpu.make_async_copy(xg.at[a, rows_of(c)], xg_out.at[a, rows_of(c)], out_sem.at[u]).start()

    def compute_forward(c):
        rows = rows_of(c)
        xc = xg[0, rows, :]
        gate = jnp.dot(xc, wg[...], preferred_element_type=F32)
        up = jnp.dot(xc, wu[...], preferred_element_type=F32)
        gate_s[rows, :] = gate
        up_s[rows, :] = up
        hidden = (gate * jax.nn.sigmoid(gate) * up).astype(BF16)
        act[rows, :] = hidden
        for q in range(T):
            part[0, q, rows, :] = jnp.dot(hidden, wd[:, q * W:(q + 1) * W], preferred_element_type=F32).astype(BF16)

    def compute_backward(c):
        rows = rows_of(c)
        grad_act = lax.dot_general(xg[1, rows, :], wd[...], NT, preferred_element_type=F32)
        gate = gate_s[rows, :]
        up = up_s[rows, :]
        sig = jax.nn.sigmoid(gate)
        term = grad_act * act[rows, :].astype(F32)
        high = term.astype(BF16)
        low = (term - high.astype(F32)).astype(BF16)
        ones = jnp.ones((8, term.shape[1]), BF16)
        sums = lax.dot_general(ones, high, NT, preferred_element_type=F32) + lax.dot_general(
            ones, low, NT, preferred_element_type=F32)
        for g in range(NG):
            vp[c * NG + g] = sums[:, g * GL:(g + 1) * GL]
        gg = (grad_act * up * sig * (1.0 + gate * (1.0 - sig))).astype(BF16)
        gu = (grad_act * gate * sig).astype(BF16)
        ggp[rows, :] = gg
        gup[rows, :] = gu
        for q in range(T):
            cut = slice(q * W, (q + 1) * W)
            part[1, q, rows, :] = (lax.dot_general(gg, wg[cut, :], NT, preferred_element_type=F32)
                                   + lax.dot_general(gu, wu[cut, :], NT, preferred_element_type=F32)).astype(BF16)

    def send_halves(w):
        a, c = w // NC, lax.rem(w, NC)
        remote(part.at[a, opp, first_half(c)], half_l.at[w], hs_sem.at[0, w], hr_sem.at[0, w], (me, right)).start()
        remote(part.at[a, opp, last_half(c)], half_r.at[w], hs_sem.at[1, w], hr_sem.at[1, w], (me, left)).start()

    def send_blocks(w):
        a, c = w // NC, lax.rem(w, NC)
        settle(half_l.at[w], hr_sem.at[0, w])
        part[a, right, first_half(c), :] = (part[a, right, first_half(c), :].astype(F32) + half_l[w].astype(F32)).astype(BF16)
        remote(part.at[a, right, rows_of(c)], blk_l.at[w], bs_sem.at[0, w], br_sem.at[0, w], (me, right)).start()
        settle(half_r.at[w], hr_sem.at[1, w])
        part[a, left, last_half(c), :] = (part[a, left, last_half(c), :].astype(F32) + half_r[w].astype(F32)).astype(BF16)
        remote(part.at[a, left, rows_of(c)], blk_r.at[w], bs_sem.at[1, w], br_sem.at[1, w], (me, left)).start()

    def give_back(w):
        a, c = w // NC, lax.rem(w, NC)
        settle(blk_l.at[w], br_sem.at[0, w])
        settle(blk_r.at[w], br_sem.at[1, w])
        fin[w] = (part[a, x, rows_of(c), :].astype(F32) + blk_l[w].astype(F32) + blk_r[w].astype(F32)).astype(BF16)

        def one(k, carry):
            r = c * OPC + k
            to = lax.rem(me - r + E, E)

            @pl.when(r > 0)
            def _():
                remote(fin.at[w, block(k)], q_out.at[a, block(me)], qs_sem.at[w], qr_sem.at[a], (to, x)).start()

            @pl.when(r == 0)
            def _():
                pltpu.make_async_copy(fin.at[w, block(0)], q_out.at[a, block(me)], qr_sem.at[a]).start()

            return carry

        lax.fori_loop(0, OPC, one, 0)

    def share_sums():
        for d in range(1, T):
            remote(vp, vx.at[d - 1], vxs_sem.at[d - 1], vxr_sem.at[d - 1], (me, lax.rem(x + d, T))).start()

    def return_sums():
        for d in range(1, T):
            settle(vx.at[d - 1], vxr_sem.at[d - 1])
        vs[...] = vp[...] + vx[0] + vx[1] + vx[2]

        def one(r, carry):
            remote(vs.at[r // OG], vr_out.at[me], vs_sem, vr_sem, (lax.rem(me - r + E, E), x)).start()
            return carry

        lax.fori_loop(1, E, one, 0)
        pltpu.make_async_copy(vs.at[0], vr_out.at[me], vr_sem).start()

    for u in range(AHEAD):
        dispatch(u)

    def step(i, carry):
        @pl.when(i + AHEAD < U)
        def _():
            dispatch(i + AHEAD)

        @pl.when(i < U)
        def _():
            spread(i)

        @pl.when(jnp.logical_and(i >= 1, i <= U))
        def _():
            forward(i - 1)

        @pl.when(jnp.logical_and(i >= U, i < 2 * U))
        def _():
            send_halves(i - U)

        @pl.when(jnp.logical_and(i >= U + 1, i <= 2 * U))
        def _():
            send_blocks(i - U - 1)

        @pl.when(i >= U + 2)
        def _():
            give_back(i - U - 2)

        @pl.when(i == U + 2)
        def _():
            return_sums()

        @pl.when(i == 2)
        def _():
            for load in loads:
                load.wait()

        @pl.when(jnp.logical_and(i >= 2, i < U + 2))
        def _():
            complete(i - 2)

        @pl.when(jnp.logical_and(i >= 2, i < NC + 2))
        def _():
            compute_forward(i - 2)

        @pl.when(jnp.logical_and(i >= NC + 2, i < U + 2))
        def _():
            compute_backward(i - 2 - NC)

        @pl.when(i == U + 1)
        def _():
            share_sums()

        return carry

    lax.fori_loop(0, 2 * U + 2, step, 0)

    def drain(u, carry):
        a, c = u // NC, lax.rem(u, NC)
        whole = fin.at[u]
        some = half_l.at[u]
        for d in range(2):
            settle(whole, xs_sem.at[d, u])
            settle(some, fs_sem.at[d, u])
            settle(some, hs_sem.at[d, u])
            settle(whole, bs_sem.at[d, u])
        settle(xg.at[a, rows_of(c)], out_sem.at[u])

        @pl.when(c > 0)
        def _():
            settle(whole, qs_sem.at[u])

        @pl.when(c == 0)
        def _():
            settle(fin.at[u, pl.ds(0, CR - C)], qs_sem.at[u])

        return carry

    lax.fori_loop(0, U, drain, 0)
    for d in range(T - 1):
        settle(vp, vxs_sem.at[d])
    settle(vr_out.at[pl.ds(0, E - 1)], vs_sem)
    settle(vr_out, vr_sem)
    for a in range(2):
        settle(s_ref.at[a, pl.ds(0, (E - 1) * C)], ds_sem.at[a])
        settle(q_out.at[a], qr_sem.at[a])


def run_kernel(E, T, C, NC, packed, w_gate, w_up, w_down):
    W = packed.shape[2]
    R = E * C
    D, FL = w_gate.shape
    CR = R // NC
    U = 2 * NC
    GL = min(128, CR)
    NG = R // GL
    dma = pltpu.SemaphoreType.DMA
    vmem = pl.BlockSpec(memory_space=pltpu.VMEM)
    hbm = pl.BlockSpec(memory_space=pl.ANY)
    flops = 2 * R * D * FL * 6
    return pl.pallas_call(
        functools.partial(moe_kernel, E, T, C, NC, GL),
        out_shape=(
            jax.ShapeDtypeStruct((2, R, D), BF16),
            jax.ShapeDtypeStruct((R, FL), BF16),
            jax.ShapeDtypeStruct((R, FL), BF16),
            jax.ShapeDtypeStruct((R, FL), BF16),
            jax.ShapeDtypeStruct((2, R, W), BF16),
            jax.ShapeDtypeStruct((E, 8, GL), F32),
        ),
        in_specs=[vmem, hbm, hbm, hbm],
        out_specs=(hbm, vmem, vmem, vmem, vmem, vmem),
        scratch_shapes=[
            pltpu.VMEM((2, R, D), BF16),
            pltpu.VMEM((2, T, R, W), BF16),
            pltpu.VMEM((R, FL), F32),
            pltpu.VMEM((R, FL), F32),
            pltpu.VMEM((D, FL), BF16),
            pltpu.VMEM((D, FL), BF16),
            pltpu.VMEM((FL, D), BF16),
            pltpu.VMEM((U, CR // 2, W), BF16),
            pltpu.VMEM((U, CR // 2, W), BF16),
            pltpu.VMEM((U, CR, W), BF16),
            pltpu.VMEM((U, CR, W), BF16),
            pltpu.VMEM((U, CR, W), BF16),
            pltpu.VMEM((NG, 8, GL), F32),
            pltpu.VMEM((T - 1, NG, 8, GL), F32),
            pltpu.VMEM((NG, 8, GL), F32),
            dma((3,)), dma((U,)), dma((2,)), dma((U,)),
            dma((2, U)), dma((2, U)), dma((2, U)), dma((2, U)), dma((2, U)), dma((2, U)),
            dma((2, U)), dma((2, U)), dma((U,)), dma((2,)),
            dma((T - 1,)), dma((T - 1,)), dma, dma,
        ],
        compiler_params=pltpu.CompilerParams(
            collective_id=0, has_side_effects=True, vmem_limit_bytes=60 * 1024 * 1024),
        cost_estimate=pl.CostEstimate(flops=flops, bytes_accessed=20 * R * D, transcendentals=2 * R * FL),
        name="moe_exchange",
    )(packed, w_gate, w_up, w_down)


def body(tokens, grad_out, gates, expert_ids, w_gate, w_up, w_down):
    E = lax.axis_size("expert")
    T = lax.axis_size("tensor")
    n, top = expert_ids.shape
    C = n * top * 4 // (3 * E)
    me = lax.axis_index("expert")
    experts = jnp.arange(E, dtype=jnp.int32)
    hit = expert_ids[:, None, :] == experts[None, :, None]
    member = jnp.any(hit, axis=2)
    gate_of = jnp.sum(jnp.where(hit, gates[:, None, :], 0.0), axis=2)
    below = (jnp.arange(n)[:, None] > jnp.arange(n)[None, :]).astype(BF16)
    earlier = jnp.dot(below, member.astype(BF16), preferred_element_type=F32).astype(jnp.int32)
    place = jnp.where(member, earlier, -1).T
    chosen = place[:, None, :] == jnp.arange(C, dtype=jnp.int32)[None, :, None]
    select = chosen.astype(BF16).reshape(E * C, n)
    weigh = jnp.where(chosen, gate_of.T[:, None, :], 0.0).reshape(E * C, n)
    slot_gate = jnp.sum(weigh, axis=1, keepdims=True)
    sent_rows = jnp.dot(select, tokens, preferred_element_type=F32).astype(BF16)
    sent_grad = (slot_gate * jnp.dot(select, grad_out, preferred_element_type=F32)).astype(BF16)
    packed = jnp.stack([sent_rows, sent_grad])
    NC = CHUNKS if E >= 64 else 2
    xg, act, ggp, gup, back, sums = run_kernel(E, T, C, NC, packed, w_gate[0], w_up[0], w_down[0])

    high = weigh.astype(BF16)
    low = (weigh - high.astype(F32)).astype(BF16)
    mixed = (lax.dot_general(high, back[0], TN, preferred_element_type=F32)
             + lax.dot_general(low, back[0], TN, preferred_element_type=F32)).astype(BF16)
    grad_tokens = lax.dot_general(select, back[1], TN, preferred_element_type=F32).astype(BF16)
    GL = sums.shape[2]
    OG = GL // C
    lane_group = lax.rem(lax.rem(experts - me + E, E), OG)
    picked = (jnp.arange(OG, dtype=jnp.int32)[None, :] == lane_group[:, None])[:, :, None]
    slot_sum = jnp.sum(jnp.where(picked, sums[:, 0, :].reshape(E, OG, C), 0.0), axis=1)
    pair_sum = jnp.sum(jnp.where(chosen, slot_sum[:, :, None], 0.0), axis=1).T
    grad_gates = jnp.sum(jnp.where(hit, pair_sum[:, :, None], 0.0), axis=1) / gates
    rows, grads = xg[0], xg[1]
    grad_down = lax.dot_general(act, grads, TN, preferred_element_type=F32).astype(BF16)
    grad_gate = lax.dot_general(rows, ggp, TN, preferred_element_type=F32).astype(BF16)
    grad_up = lax.dot_general(rows, gup, TN, preferred_element_type=F32).astype(BF16)
    return (mixed, grad_tokens, grad_gates, grad_gate[None], grad_up[None], grad_down[None])


def solution(mesh):
    placed = (
        P("expert", "tensor"),
        P("expert", "tensor"),
        P("expert", None),
        P("expert", None),
        P("expert", None, "tensor"),
        P("expert", None, "tensor"),
        P("expert", "tensor", None),
    )
    return jax.shard_map(
        body,
        mesh=mesh,
        in_specs=placed,
        out_specs=(
            P("expert", "tensor"),
            P("expert", "tensor"),
            P("expert", None),
            P("expert", None, "tensor"),
            P("expert", None, "tensor"),
            P("expert", "tensor", None),
        ),
        check_vma=False,
    )
```

```python
import functools

import jax
import jax.numpy as jnp
from jax import lax
from jax.experimental import pallas as pl
from jax.experimental.pallas import tpu as pltpu
from jax.sharding import PartitionSpec as P

F32 = jnp.float32
BF16 = jnp.bfloat16
CHUNKS = 8
AHEAD = 8
NT = (((1,), (1,)), ((), ()))
TN = (((0,), (0,)), ((), ()))


def moe_kernel(E, T, C, NC, GL, tok_hbm, grad_hbm, gates_hbm, ids_hbm, wg_hbm, wu_hbm, wd_hbm,
               gw, mg_out, gg_out,
               tok_ref, grad_ref, gates_ref, ids_ref, s0_ref, s1_ref, place_s, gate_of_s, select_s, high_s, low_s, q1, vr,
               xg, part, q0, acts, gate_s, up_s, wg, wu, wd, half_l, half_r, blk_l, blk_r, fin, vp, vx, vs,
               in_sem, w_sem, ds_sem, dr_sem, xs_sem, xr_sem, fs_sem, fr_sem, hs_sem, hr_sem,
               bs_sem, br_sem, qs_sem, qr_sem, vxs_sem, vxr_sem, vs_sem, vr_sem):
    OPC = E // NC
    CR = OPC * C
    HR = CR // 2
    W = tok_ref.shape[1]
    OG = GL // C
    NG = CR // GL
    U = 2 * NC
    me = lax.axis_index("expert")
    x = lax.axis_index("tensor")
    right = lax.rem(x + 1, T)
    left = lax.rem(x + T - 1, T)
    opp = lax.rem(x + 2, T)
    xcols = pl.ds(pl.multiple_of(x * W, W), W)
    lcols = pl.ds(pl.multiple_of(left * W, W), W)
    rcols = pl.ds(pl.multiple_of(right * W, W), W)

    small = [pltpu.make_async_copy(a, b, in_sem.at[i]) for i, (a, b) in enumerate((
        (ids_hbm, ids_ref), (gates_hbm, gates_ref), (tok_hbm, tok_ref), (grad_hbm, grad_ref)))]
    for load in small:
        load.start()
    barrier = pltpu.get_barrier_semaphore()

    def greet(r, carry):
        pl.semaphore_signal(barrier, inc=1, device_id=(lax.rem(me + r, E), x), device_id_type=pl.DeviceIdType.MESH)
        return carry

    lax.fori_loop(1, E, greet, 0)
    for d in range(1, T):
        pl.semaphore_signal(barrier, inc=1, device_id=(me, lax.rem(x + d, T)), device_id_type=pl.DeviceIdType.MESH)
    loads = [pltpu.make_async_copy(a, b, w_sem.at[i]) for i, (a, b) in enumerate(((wg_hbm, wg), (wu_hbm, wu), (wd_hbm, wd)))]
    for load in loads:
        load.start()

    for load in small:
        load.wait()
    top, n = ids_ref.shape
    expert_row = lax.broadcasted_iota(jnp.int32, (E, n), 0)
    member = jnp.zeros((E, n), F32)
    gate_of = jnp.zeros((E, n), F32)
    for k in range(top):
        hit = ids_ref[k:k + 1, :] == expert_row
        member = member + jnp.where(hit, 1.0, 0.0)
        gate_of = gate_of + jnp.where(hit, gates_ref[k:k + 1, :], 0.0)
    ahead = jnp.where(lax.broadcasted_iota(jnp.int32, (n, n), 0) < lax.broadcasted_iota(jnp.int32, (n, n), 1), 1.0, 0.0)
    earlier = jnp.dot(member.astype(BF16), ahead.astype(BF16), preferred_element_type=F32).astype(jnp.int32)
    place_s[...] = jnp.where(member > 0.5, earlier, -1)
    gate_of_s[...] = gate_of
    BR = min(128, E * C)
    EB = BR // C

    def pack(b, carry):
        own = pl.ds(pl.multiple_of(b * EB, EB), EB)
        rows = pl.ds(pl.multiple_of(b * BR, BR), BR)
        chosen = place_s[own, :][:, None, :] == lax.broadcasted_iota(jnp.int32, (EB, C, n), 1)
        select = jnp.where(chosen, 1.0, 0.0).reshape(BR, n).astype(BF16)
        weigh = jnp.where(chosen, gate_of_s[own, :][:, None, :], 0.0).reshape(BR, n)
        high = weigh.astype(BF16)
        select_s[rows, :] = select
        high_s[rows, :] = high
        low_s[rows, :] = (weigh - high.astype(F32)).astype(BF16)
        slot_gate = jnp.sum(weigh, axis=1, keepdims=True)
        s0_ref[rows, :] = jnp.dot(select, tok_ref[...], preferred_element_type=F32).astype(BF16)
        s1_ref[rows, :] = (slot_gate * jnp.dot(select, grad_ref[...], preferred_element_type=F32)).astype(BF16)
        return carry

    lax.fori_loop(0, E * C // BR, pack, 0)
    pl.semaphore_wait(barrier, E - 1 + T - 1)

    def remote(src, dst, send, recv, dev):
        return pltpu.make_async_remote_copy(src_ref=src, dst_ref=dst, send_sem=send, recv_sem=recv,
                                            device_id=dev, device_id_type=pl.DeviceIdType.MESH)

    def settle(ref, sem):
        pltpu.make_async_copy(ref, ref, sem).wait()

    def rows_of(c):
        return pl.ds(pl.multiple_of(c * CR, CR), CR)

    def first_half(c):
        return pl.ds(pl.multiple_of(c * CR, HR), HR)

    def last_half(c):
        return pl.ds(pl.multiple_of(c * CR + HR, HR), HR)

    def block(r):
        return pl.ds(pl.multiple_of(r * C, C), C)

    def dispatch(u):
        a, c = u // NC, lax.rem(u, NC)

        def one(k, carry):
            r = c * OPC + k
            to = lax.rem(me + r, E)

            for b, s_ref in enumerate((s0_ref, s1_ref)):
                @pl.when(jnp.logical_and(a == b, r > 0))
                def _():
                    remote(s_ref.at[block(to)], xg.at[b, block(r), xcols], ds_sem.at[b], dr_sem.at[u], (to, x)).start()

                @pl.when(jnp.logical_and(a == b, r == 0))
                def _():
                    pltpu.make_async_copy(s_ref.at[block(me)], xg.at[b, block(0), xcols], dr_sem.at[u]).start()

            return carry

        lax.fori_loop(0, OPC, one, 0)

    def spread(u):
        a, c = u // NC, lax.rem(u, NC)
        mine = xg.at[a, rows_of(c), xcols]
        settle(mine, dr_sem.at[u])
        remote(mine, mine, xs_sem.at[0, u], xr_sem.at[0, u], (me, right)).start()
        remote(mine, mine, xs_sem.at[1, u], xr_sem.at[1, u], (me, left)).start()

    def forward(u):
        a, c = u // NC, lax.rem(u, NC)
        settle(xg.at[a, rows_of(c), lcols], xr_sem.at[0, u])
        part_l = xg.at[a, first_half(c), lcols]
        remote(part_l, part_l, fs_sem.at[0, u], fr_sem.at[0, u], (me, right)).start()
        settle(xg.at[a, rows_of(c), rcols], xr_sem.at[1, u])
        part_r = xg.at[a, last_half(c), rcols]
        remote(part_r, part_r, fs_sem.at[1, u], fr_sem.at[1, u], (me, left)).start()

    def complete(u):
        a, c = u // NC, lax.rem(u, NC)
        ocols = pl.ds(pl.multiple_of(opp * W, W), W)
        settle(xg.at[a, first_half(c), ocols], fr_sem.at[0, u])
        settle(xg.at[a, last_half(c), ocols], fr_sem.at[1, u])

    def compute_forward(c):
        rows = rows_of(c)
        xc = xg[0, rows, :]
        gate = lax.dot_general(wg[...], xc, NT, preferred_element_type=F32)
        up = lax.dot_general(wu[...], xc, NT, preferred_element_type=F32)
        gate_s[c] = gate
        up_s[c] = up
        hidden = gate * jax.nn.sigmoid(gate) * up
        acts[0, :, rows] = hidden.astype(BF16)
        hidden = hidden.T.astype(BF16)
        for q in range(T):
            part[0, q, rows, :] = jnp.dot(hidden, wd[:, q * W:(q + 1) * W], preferred_element_type=F32).astype(BF16)

    def compute_backward(c):
        rows = rows_of(c)
        grad_act = lax.dot_general(wd[...], xg[1, rows, :], NT, preferred_element_type=F32)
        gate = gate_s[c]
        up = up_s[c]
        sig = jax.nn.sigmoid(gate)
        sums = jnp.sum(grad_act * acts[0, :, rows].astype(F32), axis=0, keepdims=True)
        sums = jnp.broadcast_to(sums, (8, CR))
        for g in range(NG):
            vp[c * NG + g] = sums[:, g * GL:(g + 1) * GL]
        gg = grad_act * up * sig * (1.0 + gate * (1.0 - sig))
        gu = grad_act * gate * sig
        acts[1, :, rows] = gg.astype(BF16)
        acts[2, :, rows] = gu.astype(BF16)
        gg = gg.T.astype(BF16)
        gu = gu.T.astype(BF16)
        for q in range(T):
            cut = slice(q * W, (q + 1) * W)
            part[1, q, rows, :] = (jnp.dot(gg, wg[:, cut], preferred_element_type=F32)
                                   + jnp.dot(gu, wu[:, cut], preferred_element_type=F32)).astype(BF16)

    def weight_grad(j):
        m, q = j // T, lax.rem(j, T)
        cols = pl.ds(pl.multiple_of(q * W, W), W)
        a = jnp.where(m == 0, 1, 0)
        gw[m, :, cols] = jnp.dot(acts[m], xg[a, :, cols], preferred_element_type=F32).astype(BF16)

    def send_halves(w):
        a, c = w // NC, lax.rem(w, NC)
        remote(part.at[a, opp, first_half(c)], half_l.at[w], hs_sem.at[0, w], hr_sem.at[0, w], (me, right)).start()
        remote(part.at[a, opp, last_half(c)], half_r.at[w], hs_sem.at[1, w], hr_sem.at[1, w], (me, left)).start()

    def send_blocks(w):
        a, c = w // NC, lax.rem(w, NC)
        settle(half_l.at[w], hr_sem.at[0, w])
        part[a, right, first_half(c), :] = (part[a, right, first_half(c), :].astype(F32) + half_l[w].astype(F32)).astype(BF16)
        remote(part.at[a, right, rows_of(c)], blk_l.at[w], bs_sem.at[0, w], br_sem.at[0, w], (me, right)).start()
        settle(half_r.at[w], hr_sem.at[1, w])
        part[a, left, last_half(c), :] = (part[a, left, last_half(c), :].astype(F32) + half_r[w].astype(F32)).astype(BF16)
        remote(part.at[a, left, rows_of(c)], blk_r.at[w], bs_sem.at[1, w], br_sem.at[1, w], (me, left)).start()

    def give_back(w):
        a, c = w // NC, lax.rem(w, NC)
        settle(blk_l.at[w], br_sem.at[0, w])
        settle(blk_r.at[w], br_sem.at[1, w])
        fin[w] = (part[a, x, rows_of(c), :].astype(F32) + blk_l[w].astype(F32) + blk_r[w].astype(F32)).astype(BF16)

        def one(k, carry):
            r = c * OPC + k
            to = lax.rem(me - r + E, E)

            for b, q_ref in enumerate((q0, q1)):
                @pl.when(jnp.logical_and(a == b, r > 0))
                def _():
                    remote(fin.at[w, block(k)], q_ref.at[block(me)], qs_sem.at[w], qr_sem.at[b], (to, x)).start()

                @pl.when(jnp.logical_and(a == b, r == 0))
                def _():
                    pltpu.make_async_copy(fin.at[w, block(0)], q_ref.at[block(me)], qr_sem.at[b]).start()

            return carry

        lax.fori_loop(0, OPC, one, 0)

    def share_sums():
        for d in range(1, T):
            remote(vp, vx.at[d - 1], vxs_sem.at[d - 1], vxr_sem.at[d - 1], (me, lax.rem(x + d, T))).start()

    def return_sums():
        for d in range(1, T):
            settle(vx.at[d - 1], vxr_sem.at[d - 1])
        vs[...] = vp[...] + vx[0] + vx[1] + vx[2]

        def one(r, carry):
            remote(vs.at[r // OG], vr.at[me], vs_sem, vr_sem, (lax.rem(me - r + E, E), x)).start()
            return carry

        lax.fori_loop(1, E, one, 0)
        pltpu.make_async_copy(vs.at[0], vr.at[me], vr_sem).start()

    for u in range(AHEAD):
        dispatch(u)

    def step(i, carry):
        @pl.when(i + AHEAD < U)
        def _():
            dispatch(i + AHEAD)

        @pl.when(i < U)
        def _():
            spread(i)

        @pl.when(jnp.logical_and(i >= 1, i <= U))
        def _():
            forward(i - 1)

        @pl.when(jnp.logical_and(i >= U, i < 2 * U))
        def _():
            send_halves(i - U)

        @pl.when(jnp.logical_and(i >= U + 1, i <= 2 * U))
        def _():
            send_blocks(i - U - 1)

        @pl.when(jnp.logical_and(i >= U + 2, i < 2 * U + 2))
        def _():
            give_back(i - U - 2)

        @pl.when(i == U + 2)
        def _():
            return_sums()

        @pl.when(i == 2)
        def _():
            for load in loads:
                load.wait()

        @pl.when(jnp.logical_and(i >= 2, i < U + 2))
        def _():
            complete(i - 2)

        @pl.when(jnp.logical_and(i >= 2, i < NC + 2))
        def _():
            compute_forward(i - 2)

        @pl.when(jnp.logical_and(i >= NC + 2, i < U + 2))
        def _():
            compute_backward(i - 2 - NC)

        @pl.when(i == U + 1)
        def _():
            share_sums()

        @pl.when(jnp.logical_and(i >= U + 2, i < U + 2 + 3 * T))
        def _():
            weight_grad(i - U - 2)

        return carry

    lax.fori_loop(0, max(2 * U + 2, U + 2 + 3 * T), step, 0)

    def drain(u, carry):
        a, c = u // NC, lax.rem(u, NC)
        whole = fin.at[u]
        some = half_l.at[u]
        for d in range(2):
            settle(whole, xs_sem.at[d, u])
            settle(some, fs_sem.at[d, u])
            settle(some, hs_sem.at[d, u])
            settle(whole, bs_sem.at[d, u])

        @pl.when(c > 0)
        def _():
            settle(whole, qs_sem.at[u])

        @pl.when(c == 0)
        def _():
            settle(fin.at[u, pl.ds(0, CR - C)], qs_sem.at[u])

        return carry

    settle(vr.at[pl.ds(0, E - 1)], vs_sem)
    settle(vr, vr_sem)
    group = lax.rem(lax.rem(lax.broadcasted_iota(jnp.int32, (E, C), 0) - me + E, E), OG)
    sums = vr[:, 0, :]
    slot_sum = jnp.zeros((E, C), F32)
    for g in range(OG):
        slot_sum = slot_sum + jnp.where(group == g, sums[:, g * C:(g + 1) * C], 0.0)
    pair_sum = jnp.zeros((E, n), F32)
    for c in range(C):
        pair_sum = pair_sum + jnp.where(place_s[...] == c, slot_sum[:, c:c + 1], 0.0)
    for k in range(top):
        terms = jnp.where(ids_ref[k:k + 1, :] == expert_row, pair_sum, 0.0)
        gg_out[k:k + 1, :] = jnp.sum(terms, axis=0, keepdims=True) / gates_ref[k:k + 1, :]
    settle(q0, qr_sem.at[0])
    mg_out[0] = (lax.dot_general(high_s[...], q0[...], TN, preferred_element_type=F32)
                    + lax.dot_general(low_s[...], q0[...], TN, preferred_element_type=F32)).astype(BF16)
    lax.fori_loop(0, U, drain, 0)
    for d in range(T - 1):
        settle(vp, vxs_sem.at[d])
    for b, s_ref in enumerate((s0_ref, s1_ref)):
        settle(s_ref.at[pl.ds(0, (E - 1) * C)], ds_sem.at[b])
    settle(q1, qr_sem.at[1])
    mg_out[1] = lax.dot_general(select_s[...], q1[...], TN, preferred_element_type=F32).astype(BF16)


def run_kernel(E, T, C, NC, tokens, grad_out, gates, ids, w_gate, w_up, w_down):
    n, W = tokens.shape
    top = ids.shape[0]
    R = E * C
    FL, D = w_gate.shape
    CR = R // NC
    U = 2 * NC
    GL = min(128, CR)
    NG = R // GL
    dma = pltpu.SemaphoreType.DMA
    vmem = pl.BlockSpec(memory_space=pltpu.VMEM)
    hbm = pl.BlockSpec(memory_space=pltpu.HBM)
    flops = 2 * R * D * FL * 9
    return pl.pallas_call(
        functools.partial(moe_kernel, E, T, C, NC, GL),
        out_shape=(
            jax.ShapeDtypeStruct((3, FL, D), BF16),
            jax.ShapeDtypeStruct((2, n, W), BF16),
            jax.ShapeDtypeStruct((top, n), F32),
        ),
        in_specs=[hbm] * 7,
        out_specs=(vmem, vmem, vmem),
        scratch_shapes=[
            pltpu.VMEM((n, W), BF16),
            pltpu.VMEM((n, W), BF16),
            pltpu.VMEM((top, n), F32),
            pltpu.VMEM((top, n), jnp.int32),
            pltpu.VMEM((R, W), BF16),
            pltpu.VMEM((R, W), BF16),
            pltpu.VMEM((E, n), jnp.int32),
            pltpu.VMEM((E, n), F32),
            pltpu.VMEM((R, n), BF16),
            pltpu.VMEM((R, n), BF16),
            pltpu.VMEM((R, n), BF16),
            pltpu.VMEM((R, W), BF16),
            pltpu.VMEM((E, 8, GL), F32),
            pltpu.VMEM((2, R, D), BF16),
            pltpu.VMEM((2, T, R, W), BF16),
            pltpu.VMEM((R, W), BF16),
            pltpu.VMEM((3, FL, R), BF16),
            pltpu.VMEM((NC, FL, CR), F32),
            pltpu.VMEM((NC, FL, CR), F32),
            pltpu.VMEM((FL, D), BF16),
            pltpu.VMEM((FL, D), BF16),
            pltpu.VMEM((FL, D), BF16),
            pltpu.VMEM((U, CR // 2, W), BF16),
            pltpu.VMEM((U, CR // 2, W), BF16),
            pltpu.VMEM((U, CR, W), BF16),
            pltpu.VMEM((U, CR, W), BF16),
            pltpu.VMEM((U, CR, W), BF16),
            pltpu.VMEM((NG, 8, GL), F32),
            pltpu.VMEM((T - 1, NG, 8, GL), F32),
            pltpu.VMEM((NG, 8, GL), F32),
            dma((4,)), dma((3,)), dma((2,)), dma((U,)),
            dma((2, U)), dma((2, U)), dma((2, U)), dma((2, U)), dma((2, U)), dma((2, U)),
            dma((2, U)), dma((2, U)), dma((U,)), dma((2,)),
            dma((T - 1,)), dma((T - 1,)), dma, dma,
        ],
        compiler_params=pltpu.CompilerParams(
            collective_id=0, has_side_effects=True, vmem_limit_bytes=44 * 1024 * 1024),
        cost_estimate=pl.CostEstimate(flops=flops, bytes_accessed=20 * R * D, transcendentals=2 * R * FL),
        name="moe_exchange",
    )(*[pltpu.with_memory_space_constraint(a, pltpu.HBM) for a in (tokens, grad_out, gates, ids, w_gate, w_up, w_down)])


def body(tokens, grad_out, gates, expert_ids, w_gate, w_up, w_down):
    E = lax.axis_size("expert")
    T = lax.axis_size("tensor")
    n, top = expert_ids.shape
    C = n * top * 4 // (3 * E)
    NC = CHUNKS if E >= 64 else 2
    weight_grads, token_outs, grad_gates = run_kernel(
        E, T, C, NC, tokens, grad_out, gates.T, expert_ids.T, w_gate[0].T, w_up[0].T, w_down[0])
    return (token_outs[0], token_outs[1], grad_gates.T, weight_grads[1].T[None], weight_grads[2].T[None], weight_grads[0][None])


def solution(mesh):
    placed = (
        P("expert", "tensor"),
        P("expert", "tensor"),
        P("expert", None),
        P("expert", None),
        P("expert", None, "tensor"),
        P("expert", None, "tensor"),
        P("expert", "tensor", None),
    )
    return jax.shard_map(
        body,
        mesh=mesh,
        in_specs=placed,
        out_specs=(
            P("expert", "tensor"),
            P("expert", "tensor"),
            P("expert", None),
            P("expert", None, "tensor"),
            P("expert", None, "tensor"),
            P("expert", "tensor", None),
        ),
        check_vma=False,
    )
```

```python
import functools

import jax
import jax.numpy as jnp
from jax import lax
from jax.experimental import pallas as pl
from jax.experimental.pallas import tpu as pltpu
from jax.sharding import PartitionSpec as P

F32 = jnp.float32
BF16 = jnp.bfloat16
CHUNKS = 8
AHEAD = 5
CORES = 2
NEAR = 1
NEAR_AT = (3, 9)
NT = (((1,), (1,)), ((), ()))
TN = (((0,), (0,)), ((), ()))


def moe_kernel(E, T, C, NC, GL, tok_hbm, grad_hbm, gates_hbm, ids_hbm, wg_hbm, wu_hbm, wd_hbm,
               gw, mg_out, gg_out,
               tok_ref, grad_ref, gates_ref, ids_ref, tx, ns, slot_gate_s, s0_ref, s1_ref, place_s, gate_of_s, select_s, high_s, low_s, q1, vr,
               xg, part, q0, acts, gate_s, up_s, wg, wu, wd, half_l, half_r, blk_l, blk_r, fin, vp, vx, vs,
               in_sem, ts_sem, tr_sem, tf_sem, tg_sem, ns_sem, w_sem, ds_sem, dr_sem, xs_sem, xr_sem, fs_sem, fr_sem, hs_sem, hr_sem,
               bs_sem, br_sem, qs_sem, qr_sem, vxs_sem, vxr_sem, vs_sem, vr_sem):
    OPC = E // NC
    CR = OPC * C
    HR = CR // 2
    W = tok_ref.shape[1]
    OG = GL // C
    NG = CR // GL
    U = 2 * NC
    me = lax.axis_index("expert")
    x = lax.axis_index("tensor")
    right = lax.rem(x + 1, T)
    left = lax.rem(x + T - 1, T)
    opp = lax.rem(x + 2, T)
    xcols = pl.ds(pl.multiple_of(x * W, W), W)
    lcols = pl.ds(pl.multiple_of(left * W, W), W)
    rcols = pl.ds(pl.multiple_of(right * W, W), W)

    small = [pltpu.make_async_copy(a, b, in_sem.at[i]) for i, (a, b) in enumerate((
        (ids_hbm, ids_ref), (gates_hbm, gates_ref), (tok_hbm, tok_ref), (grad_hbm, grad_ref),
        (tok_hbm, tx.at[0, :, xcols]), (grad_hbm, tx.at[1, :, xcols])))]
    for load in small:
        load.start()
    barrier = pltpu.get_barrier_semaphore()
    Y = OPC // CORES
    my_y = me // (NC * CORES)
    my_z = lax.rem(me // CORES, NC)
    my_core = lax.rem(me, CORES)

    order = sorted(range(NC), key=lambda d: (min(d, NC - d) * 2 + (2 * d <= NC)))
    near = [0, NC - 1][:NEAR]
    order = [d for d in order if d not in near] + near[::-1]
    FAR = NC - NEAR
    SELF = (NC - 1) * OPC

    def offset(c, k):
        dz = sum(jnp.where(c == i, d, 0) for i, d in enumerate(order))
        return k // CORES, dz, lax.rem(k, CORES)

    def expert_at(c, k):
        dy, dz, dc = offset(c, k)
        return (lax.rem(my_y + dy, Y) * NC + lax.rem(my_z + dz, NC)) * CORES + lax.rem(my_core + dc, CORES)

    def source_at(c, k):
        dy, dz, dc = offset(c, k)
        return ((lax.rem(my_y - dy + Y, Y) * NC + lax.rem(my_z - dz + NC, NC)) * CORES
                + lax.rem(my_core - dc + CORES, CORES))

    def greet(i, carry):
        r = lax.rem(i + SELF, E)
        pl.semaphore_signal(barrier, inc=1, device_id=(expert_at(r // OPC, lax.rem(r, OPC)), x),
                            device_id_type=pl.DeviceIdType.MESH)
        return carry

    lax.fori_loop(1, E, greet, 0)
    for d in range(1, T):
        pl.semaphore_signal(barrier, inc=1, device_id=(me, lax.rem(x + d, T)), device_id_type=pl.DeviceIdType.MESH)
    loads = [pltpu.make_async_copy(a, b, w_sem.at[i]) for i, (a, b) in enumerate(((wg_hbm, wg), (wu_hbm, wu), (wd_hbm, wd)))]
    for load in loads:
        load.start()

    for load in small:
        load.wait()
    top, n = ids_ref.shape
    expert_row = lax.broadcasted_iota(jnp.int32, (E, n), 0)
    member = jnp.zeros((E, n), F32)
    gate_of = jnp.zeros((E, n), F32)
    for k in range(top):
        hit = ids_ref[k:k + 1, :] == expert_row
        member = member + jnp.where(hit, 1.0, 0.0)
        gate_of = gate_of + jnp.where(hit, gates_ref[k:k + 1, :], 0.0)
    ahead = jnp.where(lax.broadcasted_iota(jnp.int32, (n, n), 0) < lax.broadcasted_iota(jnp.int32, (n, n), 1), 1.0, 0.0)
    earlier = jnp.dot(member.astype(BF16), ahead.astype(BF16), preferred_element_type=F32).astype(jnp.int32)
    place_s[...] = jnp.where(member > 0.5, earlier, -1)
    gate_of_s[...] = gate_of
    BR = min(128, E * C)
    EB = BR // C

    def pack(b, carry):
        own = pl.ds(pl.multiple_of(b * EB, EB), EB)
        rows = pl.ds(pl.multiple_of(b * BR, BR), BR)
        chosen = place_s[own, :][:, None, :] == lax.broadcasted_iota(jnp.int32, (EB, C, n), 1)
        select = jnp.where(chosen, 1.0, 0.0).reshape(BR, n).astype(BF16)
        select_s[rows, :] = select
        s0_ref[rows, :] = jnp.dot(select, tok_ref[...], preferred_element_type=F32).astype(BF16)
        return carry

    def pack_grad(b, carry):
        own = pl.ds(pl.multiple_of(b * EB, EB), EB)
        rows = pl.ds(pl.multiple_of(b * BR, BR), BR)
        chosen = place_s[own, :][:, None, :] == lax.broadcasted_iota(jnp.int32, (EB, C, n), 1)
        select = select_s[rows, :]
        weigh = jnp.where(chosen, gate_of_s[own, :][:, None, :], 0.0).reshape(BR, n)
        high = weigh.astype(BF16)
        high_s[rows, :] = high
        low_s[rows, :] = (weigh - high.astype(F32)).astype(BF16)
        slot_gate = jnp.sum(weigh, axis=1, keepdims=True)
        slot_gate_s[rows, :] = slot_gate
        s1_ref[rows, :] = (slot_gate * jnp.dot(select, grad_ref[...], preferred_element_type=F32)).astype(BF16)
        return carry

    lax.fori_loop(0, E * C // BR, pack, 0)
    pl.semaphore_wait(barrier, E - 1 + T - 1)

    def remote(src, dst, send, recv, dev):
        return pltpu.make_async_remote_copy(src_ref=src, dst_ref=dst, send_sem=send, recv_sem=recv,
                                            device_id=dev, device_id_type=pl.DeviceIdType.MESH)

    def settle(ref, sem):
        pltpu.make_async_copy(ref, ref, sem).wait()

    def rows_of(c):
        return pl.ds(pl.multiple_of(c * CR, CR), CR)

    def first_half(c):
        return pl.ds(pl.multiple_of(c * CR, HR), HR)

    def last_half(c):
        return pl.ds(pl.multiple_of(c * CR + HR, HR), HR)

    def block(r):
        return pl.ds(pl.multiple_of(r * C, C), C)

    def dispatch(u):
        a, c = u // NC, lax.rem(u, NC)

        def one(k, carry):
            r = c * OPC + k
            to = expert_at(c, k)
            for b, s_ref in enumerate((s0_ref, s1_ref)):
                @pl.when(a == b)
                def _():
                    remote(s_ref.at[block(to)], xg.at[b, block(r), xcols], ds_sem.at[b], dr_sem.at[u], (to, x)).start()

            return carry

        @pl.when(c < FAR)
        def _():
            lax.fori_loop(0, OPC, one, 0)

    HN = n // 2

    def gather_start():
        for a in range(2):
            mine = tx.at[a, :, xcols]
            remote(mine, mine, ts_sem.at[0, a], tr_sem.at[0, a], (me, right)).start()
            remote(mine, mine, ts_sem.at[1, a], tr_sem.at[1, a], (me, left)).start()

    def gather_forward():
        for a in range(2):
            settle(tx.at[a, :, lcols], tr_sem.at[0, a])
            part_l = tx.at[a, pl.ds(0, HN), lcols]
            remote(part_l, part_l, tf_sem.at[0, a], tg_sem.at[0, a], (me, right)).start()
            settle(tx.at[a, :, rcols], tr_sem.at[1, a])
            part_r = tx.at[a, pl.ds(HN, HN), rcols]
            remote(part_r, part_r, tf_sem.at[1, a], tg_sem.at[1, a], (me, left)).start()

    def pack_near():
        ocols = pl.ds(pl.multiple_of(opp * W, W), W)
        for a in range(2):
            settle(tx.at[a, pl.ds(0, HN), ocols], tg_sem.at[0, a])
            settle(tx.at[a, pl.ds(HN, HN), ocols], tg_sem.at[1, a])

        def fill(j, carry):
            to = expert_at(FAR + j // OPC, lax.rem(j, OPC))
            select = select_s[block(to), :]
            ns[0, block(j), :] = jnp.dot(select, tx[0], preferred_element_type=F32).astype(BF16)
            scaled = slot_gate_s[block(to), :] * jnp.dot(select, tx[1], preferred_element_type=F32)
            ns[1, block(j), :] = scaled.astype(BF16)
            return carry

        lax.fori_loop(0, NEAR * OPC, fill, 0)

    def dispatch_near(a):
        def one(j, carry):
            c = FAR + j // OPC
            r = FAR * OPC + j
            to = expert_at(c, lax.rem(j, OPC))

            @pl.when(r != SELF)
            def _():
                remote(ns.at[a, block(j)], xg.at[a, block(r)], ns_sem.at[a], dr_sem.at[a * NC + c], (to, x)).start()

            @pl.when(r == SELF)
            def _():
                pltpu.make_async_copy(ns.at[a, block(j)], xg.at[a, block(r)], dr_sem.at[a * NC + c]).start()

            return carry

        lax.fori_loop(0, NEAR * OPC, one, 0)

    def spread(u):
        a, c = u // NC, lax.rem(u, NC)

        @pl.when(c < FAR)
        def _():
            mine = xg.at[a, rows_of(c), xcols]
            settle(mine, dr_sem.at[u])
            remote(mine, mine, xs_sem.at[0, u], xr_sem.at[0, u], (me, right)).start()
            remote(mine, mine, xs_sem.at[1, u], xr_sem.at[1, u], (me, left)).start()

    def forward(u):
        a, c = u // NC, lax.rem(u, NC)

        @pl.when(c < FAR)
        def _():
            settle(xg.at[a, rows_of(c), lcols], xr_sem.at[0, u])
            part_l = xg.at[a, first_half(c), lcols]
            remote(part_l, part_l, fs_sem.at[0, u], fr_sem.at[0, u], (me, right)).start()
            settle(xg.at[a, rows_of(c), rcols], xr_sem.at[1, u])
            part_r = xg.at[a, last_half(c), rcols]
            remote(part_r, part_r, fs_sem.at[1, u], fr_sem.at[1, u], (me, left)).start()

    def complete(u):
        a, c = u // NC, lax.rem(u, NC)

        @pl.when(c < FAR)
        def _():
            ocols = pl.ds(pl.multiple_of(opp * W, W), W)
            settle(xg.at[a, first_half(c), ocols], fr_sem.at[0, u])
            settle(xg.at[a, last_half(c), ocols], fr_sem.at[1, u])

        @pl.when(c >= FAR)
        def _():
            settle(xg.at[a, rows_of(c)], dr_sem.at[u])

    def compute_forward(c):
        rows = rows_of(c)
        xc = xg[0, rows, :]
        gate = lax.dot_general(wg[...], xc, NT, preferred_element_type=F32)
        up = lax.dot_general(wu[...], xc, NT, preferred_element_type=F32)
        gate_s[c] = gate
        up_s[c] = up
        hidden = gate * jax.nn.sigmoid(gate) * up
        acts[0, :, rows] = hidden.astype(BF16)
        hidden = hidden.T.astype(BF16)
        for q in range(T):
            part[0, q, rows, :] = jnp.dot(hidden, wd[:, q * W:(q + 1) * W], preferred_element_type=F32).astype(BF16)

    def compute_backward(c):
        rows = rows_of(c)
        grad_act = lax.dot_general(wd[...], xg[1, rows, :], NT, preferred_element_type=F32)
        gate = gate_s[c]
        up = up_s[c]
        sig = jax.nn.sigmoid(gate)
        sums = jnp.sum(grad_act * acts[0, :, rows].astype(F32), axis=0, keepdims=True)
        sums = jnp.broadcast_to(sums, (8, CR))
        for g in range(NG):
            vp[c * NG + g] = sums[:, g * GL:(g + 1) * GL]
        gg = grad_act * up * sig * (1.0 + gate * (1.0 - sig))
        gu = grad_act * gate * sig
        acts[1, :, rows] = gg.astype(BF16)
        acts[2, :, rows] = gu.astype(BF16)
        gg = gg.T.astype(BF16)
        gu = gu.T.astype(BF16)
        for q in range(T):
            cut = slice(q * W, (q + 1) * W)
            part[1, q, rows, :] = (jnp.dot(gg, wg[:, cut], preferred_element_type=F32)
                                   + jnp.dot(gu, wu[:, cut], preferred_element_type=F32)).astype(BF16)

    def weight_grad(j):
        m, q = j // T, lax.rem(j, T)
        cols = pl.ds(pl.multiple_of(q * W, W), W)
        a = jnp.where(m == 0, 1, 0)
        gw[m, :, cols] = jnp.dot(acts[m], xg[a, :, cols], preferred_element_type=F32).astype(BF16)

    def return_chunk(w):
        p = lax.rem(w, NC)
        return jnp.where(p < FAR, FAR - 1 - p, p)

    def send_halves(w):
        a, c = w // NC, return_chunk(w)
        remote(part.at[a, opp, first_half(c)], half_l.at[w], hs_sem.at[0, w], hr_sem.at[0, w], (me, right)).start()
        remote(part.at[a, opp, last_half(c)], half_r.at[w], hs_sem.at[1, w], hr_sem.at[1, w], (me, left)).start()

    def send_blocks(w):
        a, c = w // NC, return_chunk(w)
        settle(half_l.at[w], hr_sem.at[0, w])
        part[a, right, first_half(c), :] = (part[a, right, first_half(c), :].astype(F32) + half_l[w].astype(F32)).astype(BF16)
        remote(part.at[a, right, rows_of(c)], blk_l.at[w], bs_sem.at[0, w], br_sem.at[0, w], (me, right)).start()
        settle(half_r.at[w], hr_sem.at[1, w])
        part[a, left, last_half(c), :] = (part[a, left, last_half(c), :].astype(F32) + half_r[w].astype(F32)).astype(BF16)
        remote(part.at[a, left, rows_of(c)], blk_r.at[w], bs_sem.at[1, w], br_sem.at[1, w], (me, left)).start()

    def give_back(w):
        a, c = w // NC, return_chunk(w)
        settle(blk_l.at[w], br_sem.at[0, w])
        settle(blk_r.at[w], br_sem.at[1, w])
        fin[w] = (part[a, x, rows_of(c), :].astype(F32) + blk_l[w].astype(F32) + blk_r[w].astype(F32)).astype(BF16)

        def one(k, carry):
            r = c * OPC + k
            to = source_at(c, k)

            for b, q_ref in enumerate((q0, q1)):
                @pl.when(jnp.logical_and(a == b, r != SELF))
                def _():
                    remote(fin.at[w, block(k)], q_ref.at[block(me)], qs_sem.at[w], qr_sem.at[b], (to, x)).start()

                @pl.when(jnp.logical_and(a == b, r == SELF))
                def _():
                    pltpu.make_async_copy(fin.at[w, block(k)], q_ref.at[block(me)], qr_sem.at[b]).start()

            return carry

        lax.fori_loop(0, OPC, one, 0)

    def share_sums():
        for d in range(1, T):
            remote(vp, vx.at[d - 1], vxs_sem.at[d - 1], vxr_sem.at[d - 1], (me, lax.rem(x + d, T))).start()

    def return_sums():
        for d in range(1, T):
            settle(vx.at[d - 1], vxr_sem.at[d - 1])
        vs[...] = vp[...] + vx[0] + vx[1] + vx[2]

        def one(i, carry):
            r = lax.rem(i + SELF, E)
            remote(vs.at[r // OG], vr.at[me], vs_sem, vr_sem, (source_at(r // OPC, lax.rem(r, OPC)), x)).start()
            return carry

        lax.fori_loop(1, E, one, 0)
        pltpu.make_async_copy(vs.at[SELF // OG], vr.at[me], vr_sem).start()

    gather_start()
    for u in range(min(AHEAD, FAR)):
        dispatch(u)
    lax.fori_loop(0, E * C // BR, pack_grad, 0)
    gather_forward()

    def step(i, carry):
        @pl.when(i + min(AHEAD, FAR) < U)
        def _():
            dispatch(i + min(AHEAD, FAR))

        @pl.when(i < U)
        def _():
            spread(i)

        @pl.when(jnp.logical_and(i >= 1, i <= U))
        def _():
            forward(i - 1)

        @pl.when(i == 1)
        def _():
            pack_near()

        for a, when in enumerate(NEAR_AT):
            @pl.when(i == min(when, (a + 1) * NC))
            def _():
                dispatch_near(a)

        @pl.when(jnp.logical_and(i >= U, i < 2 * U))
        def _():
            send_halves(i - U)

        @pl.when(jnp.logical_and(i >= U + 1, i <= 2 * U))
        def _():
            send_blocks(i - U - 1)

        @pl.when(jnp.logical_and(i >= U + 2, i < 2 * U + 2))
        def _():
            give_back(i - U - 2)

        @pl.when(i == U + 2)
        def _():
            return_sums()

        @pl.when(i == 2)
        def _():
            for load in loads:
                load.wait()

        @pl.when(jnp.logical_and(i >= 2, i < U + 2))
        def _():
            complete(i - 2)

        @pl.when(jnp.logical_and(i >= 2, i < NC + 2))
        def _():
            compute_forward(i - 2)

        @pl.when(jnp.logical_and(i >= NC + 2, i < U + 2))
        def _():
            compute_backward(i - 2 - NC)

        @pl.when(i == U + 1)
        def _():
            share_sums()

        @pl.when(jnp.logical_and(i >= U + 2, i < U + 2 + 3 * T))
        def _():
            weight_grad(i - U - 2)

        return carry

    lax.fori_loop(0, max(2 * U + 2, U + 2 + 3 * T), step, 0)

    def drain(u, carry):
        a, c = u // NC, return_chunk(u)
        whole = fin.at[u]
        some = half_l.at[u]
        @pl.when(lax.rem(u, NC) < FAR)
        def _():
            for d in range(2):
                settle(whole, xs_sem.at[d, u])
                settle(some, fs_sem.at[d, u])

        for d in range(2):
            settle(some, hs_sem.at[d, u])
            settle(whole, bs_sem.at[d, u])

        @pl.when(c != NC - 1)
        def _():
            settle(whole, qs_sem.at[u])

        @pl.when(c == NC - 1)
        def _():
            settle(fin.at[u, pl.ds(0, CR - C)], qs_sem.at[u])

        return carry

    settle(vr.at[pl.ds(0, E - 1)], vs_sem)
    settle(vr, vr_sem)
    expert = lax.broadcasted_iota(jnp.int32, (E, C), 0)
    away_y = lax.rem(lax.div(expert, NC * CORES) - my_y + Y, Y)
    group = away_y * CORES + lax.rem(lax.rem(expert, CORES) - my_core + CORES, CORES)
    sums = vr[:, 0, :]
    slot_sum = jnp.zeros((E, C), F32)
    for g in range(OG):
        slot_sum = slot_sum + jnp.where(group == g, sums[:, g * C:(g + 1) * C], 0.0)
    pair_sum = jnp.zeros((E, n), F32)
    for c in range(C):
        pair_sum = pair_sum + jnp.where(place_s[...] == c, slot_sum[:, c:c + 1], 0.0)
    for k in range(top):
        terms = jnp.where(ids_ref[k:k + 1, :] == expert_row, pair_sum, 0.0)
        gg_out[k:k + 1, :] = jnp.sum(terms, axis=0, keepdims=True) / gates_ref[k:k + 1, :]
    settle(q0, qr_sem.at[0])
    mg_out[0] = (lax.dot_general(high_s[...], q0[...], TN, preferred_element_type=F32)
                    + lax.dot_general(low_s[...], q0[...], TN, preferred_element_type=F32)).astype(BF16)
    lax.fori_loop(0, U, drain, 0)
    for d in range(T - 1):
        settle(vp, vxs_sem.at[d])
    for b, s_ref in enumerate((s0_ref, s1_ref)):
        settle(s_ref.at[pl.ds(0, FAR * CR)], ds_sem.at[b])
        settle(ns.at[b, pl.ds(0, NEAR * CR - C)], ns_sem.at[b])
        for d in range(2):
            settle(tx.at[b, :, xcols], ts_sem.at[d, b])
            settle(tx.at[b, pl.ds(0, HN), xcols], tf_sem.at[d, b])
    settle(q1, qr_sem.at[1])
    mg_out[1] = lax.dot_general(select_s[...], q1[...], TN, preferred_element_type=F32).astype(BF16)


def run_kernel(E, T, C, NC, tokens, grad_out, gates, ids, w_gate, w_up, w_down):
    n, W = tokens.shape
    top = ids.shape[0]
    R = E * C
    FL, D = w_gate.shape
    CR = R // NC
    U = 2 * NC
    GL = min(128, CR)
    NG = R // GL
    dma = pltpu.SemaphoreType.DMA
    vmem = pl.BlockSpec(memory_space=pltpu.VMEM)
    hbm = pl.BlockSpec(memory_space=pltpu.HBM)
    flops = 2 * R * D * FL * 9
    return pl.pallas_call(
        functools.partial(moe_kernel, E, T, C, NC, GL),
        out_shape=(
            jax.ShapeDtypeStruct((3, FL, D), BF16),
            jax.ShapeDtypeStruct((2, n, W), BF16),
            jax.ShapeDtypeStruct((top, n), F32),
        ),
        in_specs=[hbm] * 7,
        out_specs=(vmem, vmem, vmem),
        scratch_shapes=[
            pltpu.VMEM((n, W), BF16),
            pltpu.VMEM((n, W), BF16),
            pltpu.VMEM((top, n), F32),
            pltpu.VMEM((top, n), jnp.int32),
            pltpu.VMEM((2, n, D), BF16),
            pltpu.VMEM((2, NEAR * CR, D), BF16),
            pltpu.VMEM((R, 1), F32),
            pltpu.VMEM((R, W), BF16),
            pltpu.VMEM((R, W), BF16),
            pltpu.VMEM((E, n), jnp.int32),
            pltpu.VMEM((E, n), F32),
            pltpu.VMEM((R, n), BF16),
            pltpu.VMEM((R, n), BF16),
            pltpu.VMEM((R, n), BF16),
            pltpu.VMEM((R, W), BF16),
            pltpu.VMEM((E, 8, GL), F32),
            pltpu.VMEM((2, R, D), BF16),
            pltpu.VMEM((2, T, R, W), BF16),
            pltpu.VMEM((R, W), BF16),
            pltpu.VMEM((3, FL, R), BF16),
            pltpu.VMEM((NC, FL, CR), F32),
            pltpu.VMEM((NC, FL, CR), F32),
            pltpu.VMEM((FL, D), BF16),
            pltpu.VMEM((FL, D), BF16),
            pltpu.VMEM((FL, D), BF16),
            pltpu.VMEM((U, CR // 2, W), BF16),
            pltpu.VMEM((U, CR // 2, W), BF16),
            pltpu.VMEM((U, CR, W), BF16),
            pltpu.VMEM((U, CR, W), BF16),
            pltpu.VMEM((U, CR, W), BF16),
            pltpu.VMEM((NG, 8, GL), F32),
            pltpu.VMEM((T - 1, NG, 8, GL), F32),
            pltpu.VMEM((NG, 8, GL), F32),
            dma((6,)), dma((2, 2)), dma((2, 2)), dma((2, 2)), dma((2, 2)), dma((2,)), dma((3,)), dma((2,)), dma((U,)),
            dma((2, U)), dma((2, U)), dma((2, U)), dma((2, U)), dma((2, U)), dma((2, U)),
            dma((2, U)), dma((2, U)), dma((U,)), dma((2,)),
            dma((T - 1,)), dma((T - 1,)), dma, dma,
        ],
        compiler_params=pltpu.CompilerParams(
            collective_id=0, has_side_effects=True, vmem_limit_bytes=44 * 1024 * 1024),
        cost_estimate=pl.CostEstimate(flops=flops, bytes_accessed=20 * R * D, transcendentals=2 * R * FL),
        name="moe_exchange",
    )(*[pltpu.with_memory_space_constraint(a, pltpu.HBM) for a in (tokens, grad_out, gates, ids, w_gate, w_up, w_down)])


def body(tokens, grad_out, gates, expert_ids, w_gate, w_up, w_down):
    E = lax.axis_size("expert")
    T = lax.axis_size("tensor")
    n, top = expert_ids.shape
    C = n * top * 4 // (3 * E)
    NC = CHUNKS if E >= 64 else 2
    weight_grads, token_outs, grad_gates = run_kernel(
        E, T, C, NC, tokens, grad_out, gates.T, expert_ids.T, w_gate[0].T, w_up[0].T, w_down[0])
    return (token_outs[0], token_outs[1], grad_gates.T, weight_grads[1].T[None], weight_grads[2].T[None], weight_grads[0][None])


def solution(mesh):
    placed = (
        P("expert", "tensor"),
        P("expert", "tensor"),
        P("expert", None),
        P("expert", None),
        P("expert", None, "tensor"),
        P("expert", None, "tensor"),
        P("expert", "tensor", None),
    )
    return jax.shard_map(
        body,
        mesh=mesh,
        in_specs=placed,
        out_specs=(
            P("expert", "tensor"),
            P("expert", "tensor"),
            P("expert", None),
            P("expert", None, "tensor"),
            P("expert", None, "tensor"),
            P("expert", "tensor", None),
        ),
        check_vma=False,
    )
```

```python
import functools

import jax
import jax.numpy as jnp
from jax import lax
from jax.experimental import pallas as pl
from jax.experimental.pallas import tpu as pltpu
from jax.sharding import PartitionSpec as P

F32 = jnp.float32
BF16 = jnp.bfloat16
CHUNKS = 8
AHEAD = 7
CORES = 2
NEAR = 1
NEAR_AT = (3, 9)
NT = (((1,), (1,)), ((), ()))
TN = (((0,), (0,)), ((), ()))


def moe_kernel(E, T, C, NC, GL, tok_hbm, grad_hbm, gates_hbm, ids_hbm, wg_hbm, wu_hbm, wd_hbm,
               gw, mg_out, gg_out,
               tok_ref, grad_ref, gates_ref, ids_ref, tx, ns, slot_gate_s, s0_ref, s1_ref, place_s, gate_of_s, select_s, high_s, low_s, q1, vr,
               xg, part, q0, acts, gate_s, up_s, wg, wu, wd, half_l, half_r, blk_l, blk_r, fin, vp, vx, vs,
               in_sem, ts_sem, tr_sem, tf_sem, tg_sem, ns_sem, w_sem, ds_sem, dr_sem, xs_sem, xr_sem, fs_sem, fr_sem, hs_sem, hr_sem,
               bs_sem, br_sem, qs_sem, qr_sem, vxs_sem, vxr_sem, vs_sem, vr_sem):
    OPC = E // NC
    CR = OPC * C
    HR = CR // 2
    W = tok_ref.shape[1]
    OG = GL // C
    NG = CR // GL
    U = 2 * NC
    me = lax.axis_index("expert")
    x = lax.axis_index("tensor")
    right = lax.rem(x + 1, T)
    left = lax.rem(x + T - 1, T)
    opp = lax.rem(x + 2, T)
    xcols = pl.ds(pl.multiple_of(x * W, W), W)
    lcols = pl.ds(pl.multiple_of(left * W, W), W)
    rcols = pl.ds(pl.multiple_of(right * W, W), W)

    small = [pltpu.make_async_copy(a, b, in_sem.at[i]) for i, (a, b) in enumerate((
        (ids_hbm, ids_ref), (gates_hbm, gates_ref), (tok_hbm, tok_ref), (grad_hbm, grad_ref),
        (tok_hbm, tx.at[0, :, xcols]), (grad_hbm, tx.at[1, :, xcols])))]
    for load in small:
        load.start()
    barrier = pltpu.get_barrier_semaphore()
    Y = OPC // CORES
    my_y = me // (NC * CORES)
    my_z = lax.rem(me // CORES, NC)
    my_core = lax.rem(me, CORES)

    order = sorted(range(NC), key=lambda d: (min(d, NC - d) * 2 + (2 * d <= NC)))
    near = [0, NC - 1][:NEAR]
    order = [d for d in order if d not in near] + near[::-1]
    FAR = NC - NEAR
    SELF = (NC - 1) * OPC

    def offset(c, k):
        dz = sum(jnp.where(c == i, d, 0) for i, d in enumerate(order))
        return k // CORES, dz, lax.rem(k, CORES)

    def expert_at(c, k):
        dy, dz, dc = offset(c, k)
        return (lax.rem(my_y + dy, Y) * NC + lax.rem(my_z + dz, NC)) * CORES + lax.rem(my_core + dc, CORES)

    def source_at(c, k):
        dy, dz, dc = offset(c, k)
        return ((lax.rem(my_y - dy + Y, Y) * NC + lax.rem(my_z - dz + NC, NC)) * CORES
                + lax.rem(my_core - dc + CORES, CORES))

    def greet(i, carry):
        r = lax.rem(i + SELF, E)
        pl.semaphore_signal(barrier, inc=1, device_id=(expert_at(r // OPC, lax.rem(r, OPC)), x),
                            device_id_type=pl.DeviceIdType.MESH)
        return carry

    lax.fori_loop(1, E, greet, 0)
    for d in range(1, T):
        pl.semaphore_signal(barrier, inc=1, device_id=(me, lax.rem(x + d, T)), device_id_type=pl.DeviceIdType.MESH)
    loads = [pltpu.make_async_copy(a, b, w_sem.at[i]) for i, (a, b) in enumerate(((wg_hbm, wg), (wu_hbm, wu), (wd_hbm, wd)))]
    for load in loads:
        load.start()

    for load in small:
        load.wait()
    top, n = ids_ref.shape
    expert_row = lax.broadcasted_iota(jnp.int32, (E, n), 0)
    member = jnp.zeros((E, n), F32)
    gate_of = jnp.zeros((E, n), F32)
    for k in range(top):
        hit = ids_ref[k:k + 1, :] == expert_row
        member = member + jnp.where(hit, 1.0, 0.0)
        gate_of = gate_of + jnp.where(hit, gates_ref[k:k + 1, :], 0.0)
    ahead = jnp.where(lax.broadcasted_iota(jnp.int32, (n, n), 0) < lax.broadcasted_iota(jnp.int32, (n, n), 1), 1.0, 0.0)
    earlier = jnp.dot(member.astype(BF16), ahead.astype(BF16), preferred_element_type=F32).astype(jnp.int32)
    place_s[...] = jnp.where(member > 0.5, earlier, -1)
    gate_of_s[...] = gate_of
    BR = min(128, E * C)
    EB = BR // C

    def pack(b, carry):
        own = pl.ds(pl.multiple_of(b * EB, EB), EB)
        rows = pl.ds(pl.multiple_of(b * BR, BR), BR)
        chosen = place_s[own, :][:, None, :] == lax.broadcasted_iota(jnp.int32, (EB, C, n), 1)
        select = jnp.where(chosen, 1.0, 0.0).reshape(BR, n).astype(BF16)
        select_s[rows, :] = select
        s0_ref[rows, :] = jnp.dot(select, tok_ref[...], preferred_element_type=F32).astype(BF16)
        return carry

    def pack_grad(b, carry):
        own = pl.ds(pl.multiple_of(b * EB, EB), EB)
        rows = pl.ds(pl.multiple_of(b * BR, BR), BR)
        chosen = place_s[own, :][:, None, :] == lax.broadcasted_iota(jnp.int32, (EB, C, n), 1)
        select = select_s[rows, :]
        weigh = jnp.where(chosen, gate_of_s[own, :][:, None, :], 0.0).reshape(BR, n)
        high = weigh.astype(BF16)
        high_s[rows, :] = high
        low_s[rows, :] = (weigh - high.astype(F32)).astype(BF16)
        slot_gate = jnp.sum(weigh, axis=1, keepdims=True)
        slot_gate_s[rows, :] = slot_gate
        s1_ref[rows, :] = (slot_gate * jnp.dot(select, grad_ref[...], preferred_element_type=F32)).astype(BF16)
        return carry

    lax.fori_loop(0, E * C // BR, pack, 0)
    pl.semaphore_wait(barrier, E - 1 + T - 1)

    def remote(src, dst, send, recv, dev):
        return pltpu.make_async_remote_copy(src_ref=src, dst_ref=dst, send_sem=send, recv_sem=recv,
                                            device_id=dev, device_id_type=pl.DeviceIdType.MESH)

    def settle(ref, sem):
        pltpu.make_async_copy(ref, ref, sem).wait()

    def rows_of(c):
        return pl.ds(pl.multiple_of(c * CR, CR), CR)

    def first_half(c):
        return pl.ds(pl.multiple_of(c * CR, HR), HR)

    def last_half(c):
        return pl.ds(pl.multiple_of(c * CR + HR, HR), HR)

    def block(r):
        return pl.ds(pl.multiple_of(r * C, C), C)

    def dispatch(u):
        a, c = u // NC, lax.rem(u, NC)

        def one(k, carry):
            r = c * OPC + k
            to = expert_at(c, k)
            for b, s_ref in enumerate((s0_ref, s1_ref)):
                @pl.when(a == b)
                def _():
                    remote(s_ref.at[block(to)], xg.at[b, block(r), xcols], ds_sem.at[b], dr_sem.at[u], (to, x)).start()

            return carry

        @pl.when(c < FAR)
        def _():
            lax.fori_loop(0, OPC, one, 0)

    HN = n // 2

    def gather_start():
        for a in range(2):
            mine = tx.at[a, :, xcols]
            remote(mine, mine, ts_sem.at[0, a], tr_sem.at[0, a], (me, right)).start()
            remote(mine, mine, ts_sem.at[1, a], tr_sem.at[1, a], (me, left)).start()

    def gather_forward():
        for a in range(2):
            settle(tx.at[a, :, lcols], tr_sem.at[0, a])
            part_l = tx.at[a, pl.ds(0, HN), lcols]
            remote(part_l, part_l, tf_sem.at[0, a], tg_sem.at[0, a], (me, right)).start()
            settle(tx.at[a, :, rcols], tr_sem.at[1, a])
            part_r = tx.at[a, pl.ds(HN, HN), rcols]
            remote(part_r, part_r, tf_sem.at[1, a], tg_sem.at[1, a], (me, left)).start()

    def pack_near():
        ocols = pl.ds(pl.multiple_of(opp * W, W), W)
        for a in range(2):
            settle(tx.at[a, pl.ds(0, HN), ocols], tg_sem.at[0, a])
            settle(tx.at[a, pl.ds(HN, HN), ocols], tg_sem.at[1, a])

        def fill(j, carry):
            to = expert_at(FAR + j // OPC, lax.rem(j, OPC))
            select = select_s[block(to), :]
            ns[0, block(j), :] = jnp.dot(select, tx[0], preferred_element_type=F32).astype(BF16)
            scaled = slot_gate_s[block(to), :] * jnp.dot(select, tx[1], preferred_element_type=F32)
            ns[1, block(j), :] = scaled.astype(BF16)
            return carry

        lax.fori_loop(0, NEAR * OPC, fill, 0)

    def dispatch_near(a):
        def one(j, carry):
            c = FAR + j // OPC
            r = FAR * OPC + j
            to = expert_at(c, lax.rem(j, OPC))

            @pl.when(r != SELF)
            def _():
                remote(ns.at[a, block(j)], xg.at[a, block(r)], ns_sem.at[a], dr_sem.at[a * NC + c], (to, x)).start()

            @pl.when(r == SELF)
            def _():
                pltpu.make_async_copy(ns.at[a, block(j)], xg.at[a, block(r)], dr_sem.at[a * NC + c]).start()

            return carry

        lax.fori_loop(0, NEAR * OPC, one, 0)

    def spread(u):
        a, c = u // NC, lax.rem(u, NC)

        @pl.when(c < FAR)
        def _():
            mine = xg.at[a, rows_of(c), xcols]
            settle(mine, dr_sem.at[u])
            remote(mine, mine, xs_sem.at[0, u], xr_sem.at[0, u], (me, right)).start()
            remote(mine, mine, xs_sem.at[1, u], xr_sem.at[1, u], (me, left)).start()

    def forward(u):
        a, c = u // NC, lax.rem(u, NC)

        @pl.when(c < FAR)
        def _():
            settle(xg.at[a, rows_of(c), lcols], xr_sem.at[0, u])
            part_l = xg.at[a, first_half(c), lcols]
            remote(part_l, part_l, fs_sem.at[0, u], fr_sem.at[0, u], (me, right)).start()
            settle(xg.at[a, rows_of(c), rcols], xr_sem.at[1, u])
            part_r = xg.at[a, last_half(c), rcols]
            remote(part_r, part_r, fs_sem.at[1, u], fr_sem.at[1, u], (me, left)).start()

    def complete(u):
        a, c = u // NC, lax.rem(u, NC)

        @pl.when(c < FAR)
        def _():
            ocols = pl.ds(pl.multiple_of(opp * W, W), W)
            settle(xg.at[a, first_half(c), ocols], fr_sem.at[0, u])
            settle(xg.at[a, last_half(c), ocols], fr_sem.at[1, u])

        @pl.when(c >= FAR)
        def _():
            settle(xg.at[a, rows_of(c)], dr_sem.at[u])

    def compute_forward(c):
        rows = rows_of(c)
        xc = xg[0, rows, :]
        gate = lax.dot_general(wg[...], xc, NT, preferred_element_type=F32)
        up = lax.dot_general(wu[...], xc, NT, preferred_element_type=F32)
        gate_s[c] = gate
        up_s[c] = up
        hidden = gate * jax.nn.sigmoid(gate) * up
        acts[0, :, rows] = hidden.astype(BF16)
        hidden = hidden.T.astype(BF16)
        for q in range(T):
            part[0, q, rows, :] = jnp.dot(hidden, wd[:, q * W:(q + 1) * W], preferred_element_type=F32).astype(BF16)

    def compute_backward(c):
        rows = rows_of(c)
        grad_act = lax.dot_general(wd[...], xg[1, rows, :], NT, preferred_element_type=F32)
        gate = gate_s[c]
        up = up_s[c]
        sig = jax.nn.sigmoid(gate)
        sums = jnp.sum(grad_act * acts[0, :, rows].astype(F32), axis=0, keepdims=True)
        sums = jnp.broadcast_to(sums, (8, CR))
        for g in range(NG):
            vp[c * NG + g] = sums[:, g * GL:(g + 1) * GL]
        gg = grad_act * up * sig * (1.0 + gate * (1.0 - sig))
        gu = grad_act * gate * sig
        acts[1, :, rows] = gg.astype(BF16)
        acts[2, :, rows] = gu.astype(BF16)
        gg = gg.T.astype(BF16)
        gu = gu.T.astype(BF16)
        for q in range(T):
            cut = slice(q * W, (q + 1) * W)
            part[1, q, rows, :] = (jnp.dot(gg, wg[:, cut], preferred_element_type=F32)
                                   + jnp.dot(gu, wu[:, cut], preferred_element_type=F32)).astype(BF16)

    def weight_grad(j):
        m, q = j // T, lax.rem(j, T)
        cols = pl.ds(pl.multiple_of(q * W, W), W)
        a = jnp.where(m == 0, 1, 0)
        gw[m, :, cols] = jnp.dot(acts[m], xg[a, :, cols], preferred_element_type=F32).astype(BF16)

    def return_chunk(w):
        p = lax.rem(w, NC)
        return jnp.where(p < FAR, FAR - 1 - p, p)

    def send_halves(w):
        a, c = w // NC, return_chunk(w)
        remote(part.at[a, opp, first_half(c)], half_l.at[w], hs_sem.at[0, w], hr_sem.at[0, w], (me, right)).start()
        remote(part.at[a, opp, last_half(c)], half_r.at[w], hs_sem.at[1, w], hr_sem.at[1, w], (me, left)).start()

    def send_blocks(w):
        a, c = w // NC, return_chunk(w)
        settle(half_l.at[w], hr_sem.at[0, w])
        part[a, right, first_half(c), :] = (part[a, right, first_half(c), :].astype(F32) + half_l[w].astype(F32)).astype(BF16)
        remote(part.at[a, right, rows_of(c)], blk_l.at[w], bs_sem.at[0, w], br_sem.at[0, w], (me, right)).start()
        settle(half_r.at[w], hr_sem.at[1, w])
        part[a, left, last_half(c), :] = (part[a, left, last_half(c), :].astype(F32) + half_r[w].astype(F32)).astype(BF16)
        remote(part.at[a, left, rows_of(c)], blk_r.at[w], bs_sem.at[1, w], br_sem.at[1, w], (me, left)).start()

    def give_back(w):
        a, c = w // NC, return_chunk(w)
        settle(blk_l.at[w], br_sem.at[0, w])
        settle(blk_r.at[w], br_sem.at[1, w])
        fin[w] = (part[a, x, rows_of(c), :].astype(F32) + blk_l[w].astype(F32) + blk_r[w].astype(F32)).astype(BF16)

        def one(k, carry):
            r = c * OPC + k
            to = source_at(c, k)

            for b, q_ref in enumerate((q0, q1)):
                @pl.when(jnp.logical_and(a == b, r != SELF))
                def _():
                    remote(fin.at[w, block(k)], q_ref.at[block(me)], qs_sem.at[w], qr_sem.at[b], (to, x)).start()

                @pl.when(jnp.logical_and(a == b, r == SELF))
                def _():
                    pltpu.make_async_copy(fin.at[w, block(k)], q_ref.at[block(me)], qr_sem.at[b]).start()

            return carry

        lax.fori_loop(0, OPC, one, 0)

    def share_sums():
        for d in range(1, T):
            remote(vp, vx.at[d - 1], vxs_sem.at[d - 1], vxr_sem.at[d - 1], (me, lax.rem(x + d, T))).start()

    def return_sums():
        for d in range(1, T):
            settle(vx.at[d - 1], vxr_sem.at[d - 1])
        vs[...] = vp[...] + vx[0] + vx[1] + vx[2]

        def one(i, carry):
            r = lax.rem(i + SELF, E)
            remote(vs.at[r // OG], vr.at[me], vs_sem, vr_sem, (source_at(r // OPC, lax.rem(r, OPC)), x)).start()
            return carry

        lax.fori_loop(1, E, one, 0)
        pltpu.make_async_copy(vs.at[SELF // OG], vr.at[me], vr_sem).start()

    gather_start()
    for u in range(min(AHEAD, FAR)):
        dispatch(u)
    lax.fori_loop(0, E * C // BR, pack_grad, 0)
    gather_forward()

    def step(i, carry):
        @pl.when(i + min(AHEAD, FAR) < U)
        def _():
            dispatch(i + min(AHEAD, FAR))

        @pl.when(i < U)
        def _():
            spread(i)

        @pl.when(jnp.logical_and(i >= 1, i <= U))
        def _():
            forward(i - 1)

        @pl.when(i == 1)
        def _():
            pack_near()

        for a, when in enumerate(NEAR_AT):
            @pl.when(i == min(when, (a + 1) * NC))
            def _():
                dispatch_near(a)

        @pl.when(jnp.logical_and(i >= U, i < 2 * U))
        def _():
            send_halves(i - U)

        @pl.when(jnp.logical_and(i >= U + 1, i <= 2 * U))
        def _():
            send_blocks(i - U - 1)

        @pl.when(jnp.logical_and(i >= U + 2, i < 2 * U + 2))
        def _():
            give_back(i - U - 2)

        @pl.when(i == U + 2)
        def _():
            return_sums()

        @pl.when(i == 2)
        def _():
            for load in loads:
                load.wait()

        @pl.when(jnp.logical_and(i >= 2, i < U + 2))
        def _():
            complete(i - 2)

        @pl.when(jnp.logical_and(i >= 2, i < NC + 2))
        def _():
            compute_forward(i - 2)

        @pl.when(jnp.logical_and(i >= NC + 2, i < U + 2))
        def _():
            compute_backward(i - 2 - NC)

        @pl.when(i == U + 1)
        def _():
            share_sums()

        @pl.when(jnp.logical_and(i >= U + 2, i < U + 2 + 3 * T))
        def _():
            weight_grad(i - U - 2)

        return carry

    lax.fori_loop(0, max(2 * U + 2, U + 2 + 3 * T), step, 0)

    def drain(u, carry):
        a, c = u // NC, return_chunk(u)
        whole = fin.at[u]
        some = half_l.at[u]
        @pl.when(lax.rem(u, NC) < FAR)
        def _():
            for d in range(2):
                settle(whole, xs_sem.at[d, u])
                settle(some, fs_sem.at[d, u])

        for d in range(2):
            settle(some, hs_sem.at[d, u])
            settle(whole, bs_sem.at[d, u])

        @pl.when(c != NC - 1)
        def _():
            settle(whole, qs_sem.at[u])

        @pl.when(c == NC - 1)
        def _():
            settle(fin.at[u, pl.ds(0, CR - C)], qs_sem.at[u])

        return carry

    settle(vr.at[pl.ds(0, E - 1)], vs_sem)
    settle(vr, vr_sem)
    expert = lax.broadcasted_iota(jnp.int32, (E, C), 0)
    away_y = lax.rem(lax.div(expert, NC * CORES) - my_y + Y, Y)
    group = away_y * CORES + lax.rem(lax.rem(expert, CORES) - my_core + CORES, CORES)
    sums = vr[:, 0, :]
    slot_sum = jnp.zeros((E, C), F32)
    for g in range(OG):
        slot_sum = slot_sum + jnp.where(group == g, sums[:, g * C:(g + 1) * C], 0.0)
    pair_sum = jnp.zeros((E, n), F32)
    for c in range(C):
        pair_sum = pair_sum + jnp.where(place_s[...] == c, slot_sum[:, c:c + 1], 0.0)
    for k in range(top):
        terms = jnp.where(ids_ref[k:k + 1, :] == expert_row, pair_sum, 0.0)
        gg_out[k:k + 1, :] = jnp.sum(terms, axis=0, keepdims=True) / gates_ref[k:k + 1, :]
    settle(q0, qr_sem.at[0])
    mg_out[0] = (lax.dot_general(high_s[...], q0[...], TN, preferred_element_type=F32)
                    + lax.dot_general(low_s[...], q0[...], TN, preferred_element_type=F32)).astype(BF16)
    lax.fori_loop(0, U, drain, 0)
    for d in range(T - 1):
        settle(vp, vxs_sem.at[d])
    for b, s_ref in enumerate((s0_ref, s1_ref)):
        settle(s_ref.at[pl.ds(0, FAR * CR)], ds_sem.at[b])
        settle(ns.at[b, pl.ds(0, NEAR * CR - C)], ns_sem.at[b])
        for d in range(2):
            settle(tx.at[b, :, xcols], ts_sem.at[d, b])
            settle(tx.at[b, pl.ds(0, HN), xcols], tf_sem.at[d, b])
    settle(q1, qr_sem.at[1])
    mg_out[1] = lax.dot_general(select_s[...], q1[...], TN, preferred_element_type=F32).astype(BF16)


def run_kernel(E, T, C, NC, tokens, grad_out, gates, ids, w_gate, w_up, w_down):
    n, W = tokens.shape
    top = ids.shape[0]
    R = E * C
    FL, D = w_gate.shape
    CR = R // NC
    U = 2 * NC
    GL = min(128, CR)
    NG = R // GL
    dma = pltpu.SemaphoreType.DMA
    vmem = pl.BlockSpec(memory_space=pltpu.VMEM)
    hbm = pl.BlockSpec(memory_space=pltpu.HBM)
    flops = 2 * R * D * FL * 9
    return pl.pallas_call(
        functools.partial(moe_kernel, E, T, C, NC, GL),
        out_shape=(
            jax.ShapeDtypeStruct((3, FL, D), BF16),
            jax.ShapeDtypeStruct((2, n, W), BF16),
            jax.ShapeDtypeStruct((top, n), F32),
        ),
        in_specs=[hbm] * 7,
        out_specs=(vmem, vmem, vmem),
        scratch_shapes=[
            pltpu.VMEM((n, W), BF16),
            pltpu.VMEM((n, W), BF16),
            pltpu.VMEM((top, n), F32),
            pltpu.VMEM((top, n), jnp.int32),
            pltpu.VMEM((2, n, D), BF16),
            pltpu.VMEM((2, NEAR * CR, D), BF16),
            pltpu.VMEM((R, 1), F32),
            pltpu.VMEM((R, W), BF16),
            pltpu.VMEM((R, W), BF16),
            pltpu.VMEM((E, n), jnp.int32),
            pltpu.VMEM((E, n), F32),
            pltpu.VMEM((R, n), BF16),
            pltpu.VMEM((R, n), BF16),
            pltpu.VMEM((R, n), BF16),
            pltpu.VMEM((R, W), BF16),
            pltpu.VMEM((E, 8, GL), F32),
            pltpu.VMEM((2, R, D), BF16),
            pltpu.VMEM((2, T, R, W), BF16),
            pltpu.VMEM((R, W), BF16),
            pltpu.VMEM((3, FL, R), BF16),
            pltpu.VMEM((NC, FL, CR), F32),
            pltpu.VMEM((NC, FL, CR), F32),
            pltpu.VMEM((FL, D), BF16),
            pltpu.VMEM((FL, D), BF16),
            pltpu.VMEM((FL, D), BF16),
            pltpu.VMEM((U, CR // 2, W), BF16),
            pltpu.VMEM((U, CR // 2, W), BF16),
            pltpu.VMEM((U, CR, W), BF16),
            pltpu.VMEM((U, CR, W), BF16),
            pltpu.VMEM((U, CR, W), BF16),
            pltpu.VMEM((NG, 8, GL), F32),
            pltpu.VMEM((T - 1, NG, 8, GL), F32),
            pltpu.VMEM((NG, 8, GL), F32),
            dma((6,)), dma((2, 2)), dma((2, 2)), dma((2, 2)), dma((2, 2)), dma((2,)), dma((3,)), dma((2,)), dma((U,)),
            dma((2, U)), dma((2, U)), dma((2, U)), dma((2, U)), dma((2, U)), dma((2, U)),
            dma((2, U)), dma((2, U)), dma((U,)), dma((2,)),
            dma((T - 1,)), dma((T - 1,)), dma, dma,
        ],
        compiler_params=pltpu.CompilerParams(
            collective_id=0, has_side_effects=True, vmem_limit_bytes=44 * 1024 * 1024),
        cost_estimate=pl.CostEstimate(flops=flops, bytes_accessed=20 * R * D, transcendentals=2 * R * FL),
        name="moe_exchange",
    )(*[pltpu.with_memory_space_constraint(a, pltpu.HBM) for a in (tokens, grad_out, gates, ids, w_gate, w_up, w_down)])


def body(tokens, grad_out, gates, expert_ids, w_gate, w_up, w_down):
    E = lax.axis_size("expert")
    T = lax.axis_size("tensor")
    n, top = expert_ids.shape
    C = n * top * 4 // (3 * E)
    NC = CHUNKS if E >= 64 else 2
    weight_grads, token_outs, grad_gates = run_kernel(
        E, T, C, NC, tokens, grad_out, gates.T, expert_ids.T, w_gate[0].T, w_up[0].T, w_down[0])
    return (token_outs[0], token_outs[1], grad_gates.T, weight_grads[1].T[None], weight_grads[2].T[None], weight_grads[0][None])


def solution(mesh):
    placed = (
        P("expert", "tensor"),
        P("expert", "tensor"),
        P("expert", None),
        P("expert", None),
        P("expert", None, "tensor"),
        P("expert", None, "tensor"),
        P("expert", "tensor", None),
    )
    return jax.shard_map(
        body,
        mesh=mesh,
        in_specs=placed,
        out_specs=(
            P("expert", "tensor"),
            P("expert", "tensor"),
            P("expert", None),
            P("expert", None, "tensor"),
            P("expert", None, "tensor"),
            P("expert", "tensor", None),
        ),
        check_vma=False,
    )
```
